256 devices in a mesh: leaf: 16 (over y, x), sep: 8 (over z), mode: 2 (over core).
Axes of the slice: x: 4, y: 4, z: 8, core: 2. Of those that a mesh axis runs over, the one named last changes fastest.
Arguments:
- modes: bfloat16 [1024, 2048, 256], P(('leaf', 'sep'), 'mode'), may hold values from -0.125 to 0.125
- coupling: bfloat16 [1024, 2048, 256], P(('leaf', 'sep'), 'mode'), may hold values from -6 to 6
- eigenvalues: float32 [1024, 256], P(('leaf', 'sep'), 'mode'), may hold values from 200 to 4000
- separator_of: int32 [1024, 1], P(('leaf', 'sep')), may hold values from 0 to 7; in each aligned block of 8 rows (0 to 7, 8 to 15, ...) at most 2 rows name the same one
- row_offset: int32 [1024], P(('leaf', 'sep')), may hold values from 0 to 256
- stiffness: bfloat16 [8, 512, 512], P('sep', None, ('leaf', 'mode')), may hold values from -1 to 40
- start_block: bfloat16 [8, 512, 256], P('sep', ('leaf', 'mode')), may hold values from -40 to 40
- rotations: bfloat16 [8, 2, 256, 256], P('sep'), may hold values from -0.375 to 0.375
Outputs:
- subspace: bfloat16 [8, 512, 256], P('sep', ('leaf', 'mode'))
- column_norms: float32 [8, 2, 256], P('sep')
The draws below stay inside these ranges and needn't reach their ends.
Inputs may be any that keep to these rules, and one draw needn't show every extreme that they name: `separator_of`: among the 8 leaves of one device at most 2 couple to one separator, and in every draw some separator gets exactly 2 of them.
All inputs are finite; a program needn't handle non-finite values.
Results may differ from the reference program's by a relative error of at most 0.0075.
Values may be sent and summed in bfloat16 or wider, within the bound.
No kernel may reach another device: no remote copies, remote signals or barrier semaphores. Data moves between devices by JAX's collectives and lax.ppermute only.
A program may use at most 64 MiB of HBM per device.

```python
import math
import jax
import jax.numpy as jnp
import numpy as np
from jax import lax

DOF = 2048
MODES = 256
IFACE = 256
SEP_ROWS = 512
COLS = 256
LEAF_DEV = 8
CAP = 2
ITERS = 2
NLEAF = 1024
NSEP = 8


def draw_stiffness(key, part):
    split_keys = jax.random.split(key, 2)
    position = jnp.arange(SEP_ROWS, dtype=jnp.float32) / SEP_ROWS
    spread = jnp.exp(jax.random.uniform(split_keys[0], (NSEP, SEP_ROWS), jnp.float32, math.log(0.6), math.log(1.6)))
    diagonal = 2.0 * 10.0 ** position * spread
    coupled = jax.random.truncated_normal(split_keys[1], -4.0, 4.0, (NSEP, SEP_ROWS, SEP_ROWS), jnp.float32)
    coupled = coupled * (2.0 / math.sqrt(SEP_ROWS))
    identity = jnp.eye(SEP_ROWS, dtype=jnp.float32)
    return (coupled + diagonal[:, :, None] * identity[None]).astype(jnp.bfloat16)


def draw_start_block(key, part):
    split_keys = jax.random.split(key, 2)
    values = jax.random.truncated_normal(split_keys[0], -4.0, 4.0, (NSEP, SEP_ROWS, COLS), jnp.float32)
    scales = jnp.exp(jax.random.uniform(split_keys[1], (NSEP, 1, COLS), jnp.float32, 0.0, math.log(10.0)))
    return (values * scales).astype(jnp.bfloat16)


def place_ends(drawn, rng, low, top_value):
    longest = drawn.shape.index(max(drawn.shape))
    spots = []
    for shift in (0, 1):
        where = [jax.random.randint(jax.random.fold_in(rng, axis), (), 0, length) for axis, length in enumerate(drawn.shape)]
        where[longest] = (where[longest] + shift) % drawn.shape[longest]
        spots.append(tuple(where))
    return drawn.at[spots[0]].set(low).at[spots[1]].set(top_value)


def levels(rng, dims, shards, low, largest):
    def one(dim, blocks):
        steps = jax.random.uniform(jax.random.fold_in(jax.random.fold_in(rng, 6), dim), (blocks,), jnp.float32, low / len(shards), largest / len(shards))
        return jnp.repeat(jnp.exp(steps), dims[dim] // blocks).reshape((-1,) + (1,) * (len(dims) - dim - 1))

    factor_of = one(*shards[0])
    for cut in shards[1:]:
        factor_of = factor_of * one(*cut)
    return factor_of


def routed_block(own_key, own, number, rows, number_of, top, reach, skew):
    sequence = jax.random.permutation(own_key, number_of)
    heavy_load, ordinary = shares(number_of, rows * top, reach, skew, True), shares(number_of, rows * top, reach, skew, False)
    places = jnp.arange(number_of)

    def named(tallies, offset_by):
        used = int((tallies > 0).sum())
        fixed = max(1, used // 4)
        shifted = fixed + (places - fixed + offset_by * (used - fixed)) % max(1, number_of - fixed)
        return jnp.zeros((number_of,), jnp.int32).at[sequence[jnp.where(places < fixed, places, shifted)]].set(jnp.asarray(tallies, jnp.int32))

    tallies = jnp.where(number % 4 == 0, named(heavy_load, number // 4), named(ordinary, number - number // 4 - 1))
    mixed = jax.random.permutation(jax.random.fold_in(own, 3), number_of)
    giver, taker = mixed[0:number_of // 2 * 2:2], mixed[1:number_of // 2 * 2:2]
    margin = jnp.minimum(tallies[giver] - 1, reach - tallies[taker]) // 2
    margin = jnp.where((giver == sequence[0]) | (taker == sequence[0]) | (tallies[taker] == 0), 0, jnp.maximum(margin, 0))
    shifted = jax.random.randint(jax.random.fold_in(own, 4), (number_of // 2,), 0, 1 << 20) % (margin + 1)
    tallies = tallies.at[giver].add(-shifted).at[taker].add(shifted)
    items = jnp.searchsorted(jnp.cumsum(tallies), jnp.arange(rows * top), side="right").astype(jnp.int32)
    grid = items.reshape(top, rows).T
    grid = grid[jax.random.permutation(jax.random.fold_in(own, 1), rows)]
    offset_by = jax.random.randint(jax.random.fold_in(own, 2), (rows, 1), 0, top)
    return jnp.take_along_axis(grid, (jnp.arange(top)[None, :] + offset_by) % top, axis=1)


def shares(count, total, bound, lean, full):
    loads = [(1 << 20) // math.isqrt(grade ** lean) + 1 for grade in range(1, count + 1)]
    largest = bound if full else min(bound, max(-(-total // count), total * loads[0] // sum(loads)))
    least = 1 if total - largest >= count - 1 else 0
    holding, rest = [largest] + [least] * (count - 1), total - largest - least * (count - 1)
    while rest > 0:
        movable = [i for i in range(1, count) if holding[i] < largest] or [i for i in range(1, count) if holding[i] < bound]
        pool, remaining = sum([loads[i] for i in movable]), rest
        for i in movable:
            more = min(bound - holding[i], max(1, remaining * loads[i] // pool), rest)
            holding[i] = holding[i] + more
            rest = rest - more
    return np.array(holding)


def bell_draw(own_key, extent, scale, most, cuts=(), kind=jnp.bfloat16):
    level = levels(own_key, extent, cuts, -0.22, 0.18) if cuts else 1.0
    result = jax.random.normal(own_key, extent, jnp.float32) * scale * level
    return jnp.minimum(jnp.maximum(result, -most), most).astype(kind)


def setup_inputs(seed: int = 0) -> dict:
    keys = jax.random.split(jax.random.key(seed), 9)
    modes = bell_draw(keys[0], (NLEAF, DOF, MODES), DOF ** -0.5, 0.125, ((0, 128), (1, 2)))
    coupling = bell_draw(keys[1], (NLEAF, DOF, IFACE), 1.0, 6.0, ((0, 128), (1, 2)))
    eigenvalues = jnp.clip(jnp.exp(math.log(4000.0) - 2.9957323 * jax.random.uniform(keys[2], (NLEAF, MODES), jnp.float32) ** levels(keys[2], (NLEAF, MODES), ((0, 128), (1, 2)), -0.2, 0.2)), 200.0, 4000.0)
    separator_of_keys = jax.random.split(jax.random.fold_in(keys[3], 1), NLEAF // LEAF_DEV)
    separator_of_turns = jax.random.permutation(jax.random.fold_in(keys[3], 3), NLEAF // LEAF_DEV)
    separator_of = jax.vmap(lambda own, number: routed_block(jax.random.fold_in(keys[3], 2), own, number, LEAF_DEV, NSEP, 1, CAP, 2))(separator_of_keys, separator_of_turns).reshape((NLEAF, 1))
    row_offset = place_ends(jax.random.randint(keys[4], (NLEAF,), 0, SEP_ROWS - IFACE + 1), jax.random.fold_in(keys[4], 1), 0, SEP_ROWS - IFACE).astype(jnp.int32)
    stiffness = draw_stiffness(jax.random.fold_in(keys[8], 71), 0)
    start_block = draw_start_block(jax.random.fold_in(keys[8], 71), 0)
    rotations = bell_draw(keys[7], (NSEP, ITERS, COLS, COLS), COLS ** -0.5, 0.375, ((0, 8),))
    return {"modes": modes, "coupling": coupling, "eigenvalues": eigenvalues, "separator_of": separator_of, "row_offset": row_offset, "stiffness": stiffness, "start_block": start_block, "rotations": rotations}


epsilon = 1e-06

def reference(modes, coupling, eigenvalues, separator_of, row_offset, stiffness, start_block, rotations):
    highest = lax.Precision.HIGHEST

    def leaf_block(leaf_data):
        leaf_modes, leaf_coupling, leaf_eigen = leaf_data
        product = jnp.dot(leaf_coupling.T.astype(jnp.float32), leaf_modes.astype(jnp.float32), precision=highest)
        return (product / jnp.sqrt(leaf_eigen)[None, :]).astype(jnp.bfloat16)
    scaled = lax.map(leaf_block, (modes, coupling, eigenvalues))
    current = start_block
    zero_index = jnp.zeros((), jnp.int32)
    norm_list = []
    for iteration in range(ITERS):

        def add_leaf(leaf_index, accumulated):
            target = separator_of[leaf_index, 0].astype(jnp.int32)
            offset = row_offset[leaf_index].astype(jnp.int32)
            window = lax.dynamic_slice(current, (target, offset, zero_index), (1, IFACE, COLS))[0]
            weights = scaled[leaf_index].astype(jnp.float32)
            projected = jnp.dot(weights.T, window.astype(jnp.float32), precision=highest).astype(jnp.bfloat16)
            update = jnp.dot(weights, projected.astype(jnp.float32), precision=highest)
            existing = lax.dynamic_slice(accumulated, (target, offset, zero_index), (1, IFACE, COLS))
            return lax.dynamic_update_slice(accumulated, existing + update[None], (target, offset, zero_index))
        correction = lax.fori_loop(0, NLEAF, add_leaf, jnp.zeros(current.shape, jnp.float32))
        summed = jnp.einsum('srt,stc->src', stiffness.astype(jnp.float32), current.astype(jnp.float32), precision=highest) - correction
        column_scale = jnp.sqrt(lax.optimization_barrier(jnp.sum(summed * summed, 1)) / SEP_ROWS + epsilon)
        normed = (summed / column_scale[:, None, :]).astype(jnp.bfloat16)
        current = jnp.einsum('src,scd->srd', normed.astype(jnp.float32), rotations[:, iteration].astype(jnp.float32), precision=highest).astype(jnp.bfloat16)
        norm_list.append(column_scale)
    return (current, jnp.stack(norm_list, 1))
```

```python
import functools

import jax
import jax.numpy as jnp
from jax import lax
from jax.experimental import pallas as pl
from jax.experimental.pallas import tpu as pltpu
from jax.sharding import PartitionSpec as P

SEP_ROWS = 512
IFACE = 256
MODES = 256
COLS = 256
NSEP = 8
LEAF_DEV = 8
PLANE = 16
STRIP = 16
ITERS = 2
epsilon = 1e-06


def gram_kernel(target_ref, offset_ref, core_ref, own_ref, other_ref, eigen_ref, out_ref, acc_ref, pad_ref):
    leaf = pl.program_id(0)

    @pl.when(leaf == 0)
    def _():
        acc_ref[...] = jnp.zeros_like(acc_ref)

    inverse = 1.0 / jnp.sqrt(eigen_ref[0])
    scaled = ((own_ref[0] + other_ref[0]) * inverse).astype(jnp.bfloat16)
    row = lax.broadcasted_iota(jnp.int32, (SEP_ROWS, IFACE), 0)
    column = lax.broadcasted_iota(jnp.int32, (SEP_ROWS, IFACE), 1)
    placing = (row - column == offset_ref[leaf]).astype(jnp.bfloat16)
    full = jnp.dot(placing, scaled, preferred_element_type=jnp.float32).astype(jnp.bfloat16)
    pad_ref[...] = full
    core = core_ref[0]
    strips = [
        pad_ref[pl.ds(pl.multiple_of(32 * g + 16 * core, STRIP), STRIP), :] for g in range(PLANE)
    ]
    rows = jnp.concatenate(strips, axis=0)
    product = lax.dot_general(
        rows, full, (((1,), (1,)), ((), ())), preferred_element_type=jnp.float32
    )
    target = target_ref[leaf]
    acc_ref[target] = acc_ref[target] + product

    @pl.when(leaf == pl.num_programs(0) - 1)
    def _():
        for s in range(NSEP):
            for g in range(PLANE):
                out_ref[g, s] = acc_ref[s, g * STRIP : (g + 1) * STRIP, :].astype(jnp.bfloat16)


def gram(target, offset, core, own, other, eigen):
    grid_spec = pltpu.PrefetchScalarGridSpec(
        num_scalar_prefetch=3,
        grid=(LEAF_DEV,),
        in_specs=[
            pl.BlockSpec((1, IFACE, MODES), lambda l, *_: (l, 0, 0)),
            pl.BlockSpec((1, IFACE, MODES), lambda l, *_: (l, 0, 0)),
            pl.BlockSpec((1, 1, MODES), lambda l, *_: (l, 0, 0)),
        ],
        out_specs=pl.BlockSpec((PLANE, NSEP, STRIP, SEP_ROWS), lambda l, *_: (0, 0, 0, 0)),
        scratch_shapes=[
            pltpu.VMEM((NSEP, SEP_ROWS // 2, SEP_ROWS), jnp.float32),
            pltpu.VMEM((SEP_ROWS, MODES), jnp.bfloat16),
        ],
    )
    return pl.pallas_call(
        gram_kernel,
        grid_spec=grid_spec,
        out_shape=jax.ShapeDtypeStruct((PLANE, NSEP, STRIP, SEP_ROWS), jnp.bfloat16),
        name="gram",
    )(target, offset, core, own, other, eigen)


def iterate_kernel(place_ref, own_ref, other_ref, turns_ref, out_ref, norms_ref, at_ref, x_ref):
    core = place_ref[0]
    device = place_ref[1]
    for g in range(PLANE):
        first = pl.multiple_of(32 * g + 16 * core, STRIP)
        second = pl.multiple_of(32 * g + 16 * (1 - core), STRIP)
        at_ref[pl.ds(first, STRIP), :] = own_ref[g, :, :SEP_ROWS]
        at_ref[pl.ds(second, STRIP), :] = other_ref[g, :, :SEP_ROWS]
        x_ref[pl.ds(first, STRIP), :] = own_ref[g, :, SEP_ROWS:]
        x_ref[pl.ds(second, STRIP), :] = other_ref[g, :, SEP_ROWS:]
    for step in range(ITERS):
        summed = lax.dot_general(
            at_ref[...], x_ref[...], (((0,), (0,)), ((), ())), preferred_element_type=jnp.float32
        )
        scale = jnp.sqrt(jnp.sum(summed * summed, 0, keepdims=True) / SEP_ROWS + epsilon)
        norms_ref[0, pl.ds(step, 1), :] = scale
        normed = (summed / scale).astype(jnp.bfloat16)
        if step < ITERS - 1:
            x_ref[...] = jnp.dot(
                normed, turns_ref[step], preferred_element_type=jnp.float32
            ).astype(jnp.bfloat16)
        else:
            x_ref[...] = normed
            rows = x_ref[pl.ds(pl.multiple_of(16 * device, STRIP), STRIP), :]
            out_ref[0] = jnp.dot(
                rows, turns_ref[step], preferred_element_type=jnp.float32
            ).astype(jnp.bfloat16)


def iterate(place, own, other, turns):
    vmem = pl.BlockSpec(memory_space=pltpu.VMEM)
    return pl.pallas_call(
        iterate_kernel,
        in_specs=[pl.BlockSpec(memory_space=pltpu.SMEM), vmem, vmem, vmem],
        out_specs=[vmem, vmem],
        out_shape=[
            jax.ShapeDtypeStruct((1, STRIP, COLS), jnp.bfloat16),
            jax.ShapeDtypeStruct((1, ITERS, COLS), jnp.float32),
        ],
        scratch_shapes=[
            pltpu.VMEM((SEP_ROWS, SEP_ROWS), jnp.bfloat16),
            pltpu.VMEM((SEP_ROWS, COLS), jnp.bfloat16),
        ],
        name="iterate",
    )(place, own, other, turns)


SWAP = [(0, 1), (1, 0)]


def per_device(
    modes, coupling, eigenvalues, separator_of, row_offset, stiffness, start_block, rotations
):
    core = lax.axis_index("mode").astype(jnp.int32)
    device = lax.axis_index(("leaf", "mode")).astype(jnp.int32)
    other_eigen = lax.ppermute(eigenvalues, "mode", SWAP)
    eigen = jnp.where(
        core == 0,
        jnp.concatenate([eigenvalues, other_eigen], 1),
        jnp.concatenate([other_eigen, eigenvalues], 1),
    )
    own = jnp.einsum("ldw,ldm->lwm", coupling, modes, preferred_element_type=jnp.float32)
    other = lax.ppermute(own, "mode", SWAP)
    pieces = gram(
        separator_of[:, 0], row_offset, core[None], own, other, eigen[:, None, :]
    )
    got = lax.all_to_all(pieces, "leaf", split_axis=0, concat_axis=0, tiled=True)
    plane_sum = jnp.sum(got.astype(jnp.float32), 0).astype(jnp.bfloat16)
    got = lax.all_to_all(plane_sum, "sep", split_axis=0, concat_axis=0, tiled=True)
    correction = jnp.sum(got.astype(jnp.float32), 0)
    columns = (stiffness[0].T.astype(jnp.float32) - correction).astype(jnp.bfloat16)
    packed = jnp.concatenate([columns, start_block[0]], 1)
    mine = lax.all_to_all(
        jnp.broadcast_to(packed[None], (PLANE, *packed.shape)),
        "leaf",
        split_axis=0,
        concat_axis=0,
        tiled=True,
    )
    theirs = lax.ppermute(mine, "mode", SWAP)
    return tuple(iterate(jnp.stack([core, device]), mine, theirs, rotations[0]))


def solution(mesh):
    in_specs = (
        P(("leaf", "sep"), "mode", None),
        P(("leaf", "sep"), "mode", None),
        P(("leaf", "sep"), "mode"),
        P(("leaf", "sep"), None),
        P(("leaf", "sep")),
        P("sep", None, ("leaf", "mode")),
        P("sep", ("leaf", "mode"), None),
        P("sep", None, None, None),
    )
    out_specs = (P("sep", ("leaf", "mode"), None), P("sep", None, None))
    return jax.shard_map(
        per_device, mesh=mesh, in_specs=in_specs, out_specs=out_specs, check_vma=False
    )
```

```python
import functools

import jax
import jax.numpy as jnp
from jax import lax
from jax.experimental import pallas as pl
from jax.experimental.pallas import tpu as pltpu
from jax.sharding import PartitionSpec as P

SEP_ROWS = 512
IFACE = 256
MODES = 256
COLS = 256
NSEP = 8
LEAF_DEV = 8
PLANE = 16
SIDE = 4
GROUPS = 8
STRIP = 16
ITERS = 2
epsilon = 1e-06


def place_of(d, e, first, second, core):
    one = (first + d) & (SIDE - 1)
    two = (second + e) & (SIDE - 1)
    return jnp.where(core == 0, two * SIDE + one, one * SIDE + two)


def gram_kernel(target_ref, offset_ref, place_ref, own_ref, other_ref, eigen_ref, *refs):
    out_refs, pad_ref = refs[:SIDE], refs[SIDE]
    core, first, second = place_ref[0], place_ref[1], place_ref[2]
    row = lax.broadcasted_iota(jnp.int32, (SEP_ROWS, IFACE), 0)
    column = lax.broadcasted_iota(jnp.int32, (SEP_ROWS, IFACE), 1)
    distance = row - column
    pad_ref[LEAF_DEV] = jnp.zeros((SEP_ROWS, MODES), jnp.bfloat16)
    for leaf in range(LEAF_DEV):
        inverse = 1.0 / jnp.sqrt(eigen_ref[leaf : leaf + 1, :])
        scaled = ((own_ref[leaf] + other_ref[leaf]) * inverse).astype(jnp.bfloat16)
        placing = (distance == offset_ref[leaf]).astype(jnp.bfloat16)
        pad_ref[leaf] = jnp.dot(placing, scaled, preferred_element_type=jnp.float32).astype(
            jnp.bfloat16
        )
    starts = [
        pl.multiple_of(32 * place_of(d, e, first, second, core) + 16 * core, STRIP)
        for d in range(SIDE)
        for e in range(SIDE)
    ]
    for s in range(NSEP):
        slots = [jnp.int32(LEAF_DEV), jnp.int32(LEAF_DEV)]
        for leaf in range(LEAF_DEV):
            hit = target_ref[leaf] == s
            later = hit & (slots[0] < LEAF_DEV)
            slots[1] = jnp.where(later, leaf, slots[1])
            slots[0] = jnp.where(hit & jnp.logical_not(later), leaf, slots[0])
        total = None
        for slot in slots:
            rows = jnp.concatenate([pad_ref[slot, pl.ds(x, STRIP), :] for x in starts], axis=0)
            product = lax.dot_general(
                rows, pad_ref[slot], (((1,), (1,)), ((), ())), preferred_element_type=jnp.float32
            )
            total = product if total is None else total + product
        total = total.astype(jnp.bfloat16)
        for d in range(SIDE):
            for e in range(SIDE):
                k = (d * SIDE + e) * STRIP
                out_refs[d][e, s] = total[k : k + STRIP, :]


VMEM = pl.BlockSpec(memory_space=pltpu.VMEM)
SMEM = pl.BlockSpec(memory_space=pltpu.SMEM)


def gram(target, offset, place, own, other, eigen):
    piece = jax.ShapeDtypeStruct((SIDE, NSEP, STRIP, SEP_ROWS), jnp.bfloat16)
    return pl.pallas_call(
        gram_kernel,
        in_specs=[SMEM, SMEM, SMEM, VMEM, VMEM, VMEM],
        out_specs=[VMEM] * SIDE,
        out_shape=[piece] * SIDE,
        scratch_shapes=[pltpu.VMEM((LEAF_DEV + 1, SEP_ROWS, MODES), jnp.bfloat16)],
        name="gram",
    )(target, offset, place, own, other, eigen)


def total_kernel(count, *refs):
    sources, outs = refs[:count], refs[count:]
    for k, out_ref in enumerate(outs):
        for s in range(NSEP):
            value = sum(ref[k, s].astype(jnp.float32) for ref in sources)
            out_ref[s] = value.astype(jnp.bfloat16)


def total(pieces):
    lead = pieces[0].shape[0]
    return pl.pallas_call(
        functools.partial(total_kernel, len(pieces)),
        in_specs=[VMEM] * len(pieces),
        out_specs=[VMEM] * lead,
        out_shape=[jax.ShapeDtypeStruct(pieces[0].shape[1:], jnp.bfloat16)] * lead,
        name="total",
    )(*pieces)


def iterate_kernel(place_ref, own_ref, other_ref, turns_ref, out_ref, norms_ref, at_ref, x_ref):
    core = place_ref[0]
    device = place_ref[1]
    for g in range(PLANE):
        first = pl.multiple_of(32 * g + 16 * core, STRIP)
        second = pl.multiple_of(32 * g + 16 * (1 - core), STRIP)
        at_ref[pl.ds(first, STRIP), :] = own_ref[g, :, :SEP_ROWS]
        at_ref[pl.ds(second, STRIP), :] = other_ref[g, :, :SEP_ROWS]
        x_ref[pl.ds(first, STRIP), :] = own_ref[g, :, SEP_ROWS:]
        x_ref[pl.ds(second, STRIP), :] = other_ref[g, :, SEP_ROWS:]
    for step in range(ITERS):
        summed = lax.dot_general(
            at_ref[...], x_ref[...], (((0,), (0,)), ((), ())), preferred_element_type=jnp.float32
        )
        scale = jnp.sqrt(jnp.sum(summed * summed, 0, keepdims=True) / SEP_ROWS + epsilon)
        norms_ref[0, pl.ds(step, 1), :] = scale
        normed = (summed / scale).astype(jnp.bfloat16)
        if step < ITERS - 1:
            x_ref[...] = jnp.dot(
                normed, turns_ref[step], preferred_element_type=jnp.float32
            ).astype(jnp.bfloat16)
        else:
            x_ref[...] = normed
            rows = x_ref[pl.ds(pl.multiple_of(16 * device, STRIP), STRIP), :]
            out_ref[0] = jnp.dot(
                rows, turns_ref[step], preferred_element_type=jnp.float32
            ).astype(jnp.bfloat16)


def iterate(place, own, other, turns):
    vmem = pl.BlockSpec(memory_space=pltpu.VMEM)
    return pl.pallas_call(
        iterate_kernel,
        in_specs=[pl.BlockSpec(memory_space=pltpu.SMEM), vmem, vmem, vmem],
        out_specs=[vmem, vmem],
        out_shape=[
            jax.ShapeDtypeStruct((1, STRIP, COLS), jnp.bfloat16),
            jax.ShapeDtypeStruct((1, ITERS, COLS), jnp.float32),
        ],
        scratch_shapes=[
            pltpu.VMEM((SEP_ROWS, SEP_ROWS), jnp.bfloat16),
            pltpu.VMEM((SEP_ROWS, COLS), jnp.bfloat16),
        ],
        name="iterate",
    )(place, own, other, turns)


SWAP = [(0, 1), (1, 0)]
AXES = ("leaf", "sep", "mode")


def index_of(y, x, z, core):
    return ((y * SIDE + x) * GROUPS + z) * 2 + core


def plane_steps(step, stage):
    pairs = []
    for y in range(SIDE):
        for x in range(SIDE):
            for z in range(GROUPS):
                for core in range(2):
                    along_x = (core + stage) % 2 == 0
                    to = (y, (x + step) % SIDE) if along_x else ((y + step) % SIDE, x)
                    pairs.append((index_of(y, x, z, core), index_of(*to, z, core)))
    return pairs


def scatter_stage(pieces, stage):
    got = [lax.ppermute(pieces[d], AXES, plane_steps(d, stage)) for d in range(1, SIDE)]
    return [pieces[0], *got]


def per_device(
    modes, coupling, eigenvalues, separator_of, row_offset, stiffness, start_block, rotations
):
    core = lax.axis_index("mode").astype(jnp.int32)
    device = lax.axis_index(("leaf", "mode")).astype(jnp.int32)
    other_eigen = lax.ppermute(eigenvalues, "mode", SWAP)
    eigen = jnp.where(
        core == 0,
        jnp.concatenate([eigenvalues, other_eigen], 1),
        jnp.concatenate([other_eigen, eigenvalues], 1),
    )
    own = jnp.einsum("ldw,ldm->lwm", coupling, modes, preferred_element_type=jnp.float32)
    other = lax.ppermute(own, "mode", SWAP)
    leaf = lax.axis_index("leaf").astype(jnp.int32)
    y, x = leaf >> 2, leaf & 3
    place = jnp.stack([core, jnp.where(core == 0, x, y), jnp.where(core == 0, y, x)])
    pieces = gram(separator_of[:, 0], row_offset, place, own, other, eigen)
    pieces = total(scatter_stage(pieces, 0))
    pieces = [piece[None] for piece in pieces]
    (plane_sum,) = total(scatter_stage(pieces, 1))
    got = lax.all_to_all(plane_sum, "sep", split_axis=0, concat_axis=0, tiled=True)
    correction = jnp.sum(got.astype(jnp.float32), 0)
    columns = (stiffness[0].T.astype(jnp.float32) - correction).astype(jnp.bfloat16)
    packed = jnp.concatenate([columns, start_block[0]], 1)
    mine = lax.all_to_all(
        jnp.broadcast_to(packed[None], (PLANE, *packed.shape)),
        "leaf",
        split_axis=0,
        concat_axis=0,
        tiled=True,
    )
    theirs = lax.ppermute(mine, "mode", SWAP)
    return tuple(iterate(jnp.stack([core, device]), mine, theirs, rotations[0]))


def solution(mesh):
    in_specs = (
        P(("leaf", "sep"), "mode", None),
        P(("leaf", "sep"), "mode", None),
        P(("leaf", "sep"), "mode"),
        P(("leaf", "sep"), None),
        P(("leaf", "sep")),
        P("sep", None, ("leaf", "mode")),
        P("sep", ("leaf", "mode"), None),
        P("sep", None, None, None),
    )
    out_specs = (P("sep", ("leaf", "mode"), None), P("sep", None, None))
    return jax.shard_map(
        per_device, mesh=mesh, in_specs=in_specs, out_specs=out_specs, check_vma=False
    )
```

```python
import functools

import jax
import jax.numpy as jnp
from jax import lax
from jax.experimental import pallas as pl
from jax.experimental.pallas import tpu as pltpu
from jax.sharding import PartitionSpec as P

SEP_ROWS = 512
IFACE = 256
MODES = 256
COLS = 256
NSEP = 8
LEAF_DEV = 8
PLANE = 16
SIDE = 4
GROUPS = 8
STRIP = 16
ITERS = 2
epsilon = 1e-06


def place_of(d, e, first, second, core):
    one = (first + d) & (SIDE - 1)
    two = (second + e) & (SIDE - 1)
    return jnp.where(core == 0, two * SIDE + one, one * SIDE + two)


def gram_kernel(target_ref, offset_ref, place_ref, own_ref, other_ref, eigen_ref, *refs):
    out_refs, pad_ref = refs[: 2 * SIDE], refs[2 * SIDE]
    core, first, second = place_ref[0], place_ref[1], place_ref[2]
    row = lax.broadcasted_iota(jnp.int32, (SEP_ROWS, IFACE), 0)
    column = lax.broadcasted_iota(jnp.int32, (SEP_ROWS, IFACE), 1)
    distance = row - column
    pad_ref[LEAF_DEV] = jnp.zeros((SEP_ROWS, MODES), jnp.bfloat16)
    for leaf in range(LEAF_DEV):
        inverse = 1.0 / jnp.sqrt(eigen_ref[leaf : leaf + 1, :])
        scaled = ((own_ref[leaf] + other_ref[leaf]) * inverse).astype(jnp.bfloat16)
        placing = (distance == offset_ref[leaf]).astype(jnp.bfloat16)
        pad_ref[leaf] = jnp.dot(placing, scaled, preferred_element_type=jnp.float32).astype(
            jnp.bfloat16
        )
    starts = [
        pl.multiple_of(32 * place_of(d, e, first, second, core) + 16 * core, STRIP)
        for d in range(SIDE)
        for e in range(SIDE)
    ]
    for s in range(NSEP):
        slots = [jnp.int32(LEAF_DEV), jnp.int32(LEAF_DEV)]
        for leaf in range(LEAF_DEV):
            hit = target_ref[leaf] == s
            later = hit & (slots[0] < LEAF_DEV)
            slots[1] = jnp.where(later, leaf, slots[1])
            slots[0] = jnp.where(hit & jnp.logical_not(later), leaf, slots[0])
        total = None
        for slot in slots:
            rows = jnp.concatenate([pad_ref[slot, pl.ds(x, STRIP), :] for x in starts], axis=0)
            product = lax.dot_general(
                rows, pad_ref[slot], (((1,), (1,)), ((), ())), preferred_element_type=jnp.float32
            )
            total = product if total is None else total + product
        total = total.astype(jnp.bfloat16)
        for d in range(SIDE):
            for e in range(SIDE):
                k = (d * SIDE + e) * STRIP
                out_refs[2 * d + e // 2][e % 2, s] = total[k : k + STRIP, :]


VMEM = pl.BlockSpec(memory_space=pltpu.VMEM)
SMEM = pl.BlockSpec(memory_space=pltpu.SMEM)


def gram(target, offset, place, own, other, eigen):
    piece = jax.ShapeDtypeStruct((2, NSEP, STRIP, SEP_ROWS), jnp.bfloat16)
    return pl.pallas_call(
        gram_kernel,
        in_specs=[SMEM, SMEM, SMEM, VMEM, VMEM, VMEM],
        out_specs=[VMEM] * (2 * SIDE),
        out_shape=[piece] * (2 * SIDE),
        scratch_shapes=[pltpu.VMEM((LEAF_DEV + 1, SEP_ROWS, MODES), jnp.bfloat16)],
        name="gram",
    )(target, offset, place, own, other, eigen)


def iterate_kernel(place_ref, own_ref, other_ref, turns_ref, out_ref, norms_ref, at_ref, x_ref):
    core = place_ref[0]
    device = place_ref[1]
    for g in range(PLANE):
        first = pl.multiple_of(32 * g + 16 * core, STRIP)
        second = pl.multiple_of(32 * g + 16 * (1 - core), STRIP)
        at_ref[pl.ds(first, STRIP), :] = own_ref[g, :, :SEP_ROWS]
        at_ref[pl.ds(second, STRIP), :] = other_ref[g, :, :SEP_ROWS]
        x_ref[pl.ds(first, STRIP), :] = own_ref[g, :, SEP_ROWS:]
        x_ref[pl.ds(second, STRIP), :] = other_ref[g, :, SEP_ROWS:]
    for step in range(ITERS):
        summed = lax.dot_general(
            at_ref[...], x_ref[...], (((0,), (0,)), ((), ())), preferred_element_type=jnp.float32
        )
        scale = jnp.sqrt(jnp.sum(summed * summed, 0, keepdims=True) / SEP_ROWS + epsilon)
        norms_ref[0, pl.ds(step, 1), :] = scale
        normed = (summed / scale).astype(jnp.bfloat16)
        if step < ITERS - 1:
            x_ref[...] = jnp.dot(
                normed, turns_ref[step], preferred_element_type=jnp.float32
            ).astype(jnp.bfloat16)
        else:
            x_ref[...] = normed
            rows = x_ref[pl.ds(pl.multiple_of(16 * device, STRIP), STRIP), :]
            out_ref[0] = jnp.dot(
                rows, turns_ref[step], preferred_element_type=jnp.float32
            ).astype(jnp.bfloat16)


def iterate(place, own, other, turns):
    vmem = pl.BlockSpec(memory_space=pltpu.VMEM)
    return pl.pallas_call(
        iterate_kernel,
        in_specs=[pl.BlockSpec(memory_space=pltpu.SMEM), vmem, vmem, vmem],
        out_specs=[vmem, vmem],
        out_shape=[
            jax.ShapeDtypeStruct((1, STRIP, COLS), jnp.bfloat16),
            jax.ShapeDtypeStruct((1, ITERS, COLS), jnp.float32),
        ],
        scratch_shapes=[
            pltpu.VMEM((SEP_ROWS, SEP_ROWS), jnp.bfloat16),
            pltpu.VMEM((SEP_ROWS, COLS), jnp.bfloat16),
        ],
        name="iterate",
    )(place, own, other, turns)


SWAP = [(0, 1), (1, 0)]
AXES = ("leaf", "sep", "mode")


def index_of(y, x, z, core):
    return ((y * SIDE + x) * GROUPS + z) * 2 + core


def plane_steps(step, stage):
    pairs = []
    for y in range(SIDE):
        for x in range(SIDE):
            for z in range(GROUPS):
                for core in range(2):
                    along_x = (core + stage) % 2 == 0
                    to = (y, (x + step) % SIDE) if along_x else ((y + step) % SIDE, x)
                    pairs.append((index_of(y, x, z, core), index_of(*to, z, core)))
    return pairs


def add(*terms):
    return sum(term.astype(jnp.float32) for term in terms).astype(jnp.bfloat16)


def ring_scatter(pieces, stage):
    up = functools.partial(lax.ppermute, axis_name=AXES, perm=plane_steps(1, stage))
    down = functools.partial(lax.ppermute, axis_name=AXES, perm=plane_steps(SIDE - 1, stage))
    own, ahead, opposite, behind = pieces
    relay_down, relay_up = down(opposite[0]), up(opposite[1])
    direct_down, direct_up = down(behind[1]), up(ahead[0])
    last_down, last_up = down(add(behind[0], relay_down)), up(add(ahead[1], relay_up))
    return (own[0], direct_up, last_down), (own[1], last_up, direct_down)


def per_device(
    modes, coupling, eigenvalues, separator_of, row_offset, stiffness, start_block, rotations
):
    core = lax.axis_index("mode").astype(jnp.int32)
    device = lax.axis_index(("leaf", "mode")).astype(jnp.int32)
    other_eigen = lax.ppermute(eigenvalues, "mode", SWAP)
    eigen = jnp.where(
        core == 0,
        jnp.concatenate([eigenvalues, other_eigen], 1),
        jnp.concatenate([other_eigen, eigenvalues], 1),
    )
    own = jnp.einsum("ldw,ldm->lwm", coupling, modes, preferred_element_type=jnp.float32)
    other = lax.ppermute(own, "mode", SWAP)
    leaf = lax.axis_index("leaf").astype(jnp.int32)
    y, x = leaf >> 2, leaf & 3
    place = jnp.stack([core, jnp.where(core == 0, x, y), jnp.where(core == 0, y, x)])
    halves = gram(separator_of[:, 0], row_offset, place, own, other, eigen)
    terms = ring_scatter([halves[2 * d : 2 * d + 2] for d in range(SIDE)], 0)
    strips = [add(*[term[e % 2] for term in terms[e // 2]]) for e in range(SIDE)]
    half = NSEP // 2
    terms = ring_scatter([(strip[:half], strip[half:]) for strip in strips], 1)
    plane_sum = jnp.concatenate([add(*terms[0]), add(*terms[1])], 0)
    got = lax.all_to_all(plane_sum, "sep", split_axis=0, concat_axis=0, tiled=True)
    correction = jnp.sum(got.astype(jnp.float32), 0)
    columns = (stiffness[0].T.astype(jnp.float32) - correction).astype(jnp.bfloat16)
    packed = jnp.concatenate([columns, start_block[0]], 1)
    mine = lax.all_to_all(
        jnp.broadcast_to(packed[None], (PLANE, *packed.shape)),
        "leaf",
        split_axis=0,
        concat_axis=0,
        tiled=True,
    )
    theirs = lax.ppermute(mine, "mode", SWAP)
    return tuple(iterate(jnp.stack([core, device]), mine, theirs, rotations[0]))


def solution(mesh):
    in_specs = (
        P(("leaf", "sep"), "mode", None),
        P(("leaf", "sep"), "mode", None),
        P(("leaf", "sep"), "mode"),
        P(("leaf", "sep"), None),
        P(("leaf", "sep")),
        P("sep", None, ("leaf", "mode")),
        P("sep", ("leaf", "mode"), None),
        P("sep", None, None, None),
    )
    out_specs = (P("sep", ("leaf", "mode"), None), P("sep", None, None))
    return jax.shard_map(
        per_device, mesh=mesh, in_specs=in_specs, out_specs=out_specs, check_vma=False
    )
```

```python
import functools

import jax
import jax.numpy as jnp
from jax import lax
from jax.experimental import pallas as pl
from jax.experimental.pallas import tpu as pltpu
from jax.sharding import PartitionSpec as P

SEP_ROWS = 512
IFACE = 256
MODES = 256
COLS = 256
NSEP = 8
LEAF_DEV = 8
PLANE = 16
TILES = 18
STRIP = 16
ITERS = 2
epsilon = 1e-06


def gram_kernel(target_ref, offset_ref, core_ref, own_ref, other_ref, eigen_ref, out_ref, pad_ref):
    core = core_ref[0]
    row = lax.broadcasted_iota(jnp.int32, (SEP_ROWS, IFACE), 0)
    column = lax.broadcasted_iota(jnp.int32, (SEP_ROWS, IFACE), 1)
    distance = row - column
    pad_ref[LEAF_DEV] = jnp.zeros((SEP_ROWS, MODES), jnp.bfloat16)
    for leaf in range(LEAF_DEV):
        inverse = 1.0 / jnp.sqrt(eigen_ref[leaf : leaf + 1, :])
        scaled = ((own_ref[leaf] + other_ref[leaf]) * inverse).astype(jnp.bfloat16)
        placing = (distance == offset_ref[leaf]).astype(jnp.bfloat16)
        pad_ref[leaf] = jnp.dot(placing, scaled, preferred_element_type=jnp.float32).astype(
            jnp.bfloat16
        )
    starts = [pl.multiple_of(32 * g + 16 * core, STRIP) for g in range(PLANE)]
    for s in range(NSEP):
        slots = [jnp.int32(LEAF_DEV), jnp.int32(LEAF_DEV)]
        for leaf in range(LEAF_DEV):
            hit = target_ref[leaf] == s
            later = hit & (slots[0] < LEAF_DEV)
            slots[1] = jnp.where(later, leaf, slots[1])
            slots[0] = jnp.where(hit & jnp.logical_not(later), leaf, slots[0])
        total = None
        for slot in slots:
            rows = jnp.concatenate([pad_ref[slot, pl.ds(x, STRIP), :] for x in starts], axis=0)
            product = lax.dot_general(
                rows, pad_ref[slot], (((1,), (1,)), ((), ())), preferred_element_type=jnp.float32
            )
            total = product if total is None else total + product
        lane = 32 * (s % 4)
        for g in range(PLANE):
            strip = total[g * STRIP : (g + 1) * STRIP, :]
            window = jnp.roll(strip, -32 * g, axis=1) if g else strip
            out_ref[g, 2 * s] = window[:, :128].astype(jnp.bfloat16)
            out_ref[g, 2 * s + 1] = window[:, 128:256].astype(jnp.bfloat16)
            rest = window[:, 256:384]
            rest = jnp.roll(rest, lane, axis=1) if lane else rest
            out_ref[g, 16 + s // 4, :, lane : lane + 32] = rest[:, lane : lane + 32].astype(
                jnp.bfloat16
            )


VMEM = pl.BlockSpec(memory_space=pltpu.VMEM)
SMEM = pl.BlockSpec(memory_space=pltpu.SMEM)


def gram(target, offset, core, own, other, eigen):
    return pl.pallas_call(
        gram_kernel,
        in_specs=[SMEM, SMEM, SMEM, VMEM, VMEM, VMEM],
        out_specs=VMEM,
        out_shape=jax.ShapeDtypeStruct((PLANE, TILES, STRIP, 128), jnp.bfloat16),
        scratch_shapes=[pltpu.VMEM((LEAF_DEV + 1, SEP_ROWS, MODES), jnp.bfloat16)],
        name="gram",
    )(target, offset, core, own, other, eigen)


def iterate_kernel(
    place_ref, own_ref, other_ref, turns_ref, out_ref, norms_ref, kt_ref, m_ref, high_ref, low_ref, x_ref
):
    core, device, sep = place_ref[0], place_ref[1], place_ref[2]
    lane = lax.broadcasted_iota(jnp.int32, (STRIP, 128), 1)
    halved = jnp.where(lane < 32, 0.5, 1.0)
    rest_weight = jnp.where(lane < 32, 0.5, 0.0)
    back = (128 - 32 * (sep & 3)) & 127
    for ref, offset in ((own_ref, 16 * core), (other_ref, 16 * (1 - core))):
        for g in range(PLANE):
            rows = pl.ds(pl.multiple_of(32 * g + offset, STRIP), STRIP)
            kt_ref[rows, :] = ref[g, :, :512]
            x_ref[rows, :] = ref[g, :, 512:768]
            first = ref[g, :, 768:896].astype(jnp.float32) + ref[g, :, 1152:1280].astype(jnp.float32)
            second = ref[g, :, 896:1024].astype(jnp.float32)
            rest = pltpu.roll(ref[g, :, 1024:1152].astype(jnp.float32), back, axis=1)
            window = jnp.concatenate(
                [first * halved, second, rest * rest_weight, jnp.zeros_like(second)], axis=1
            )
            m_ref[rows, :] = jnp.roll(window, 32 * g, axis=1) if g else window
    half = m_ref[...]
    operator = jnp.transpose(kt_ref[...].astype(jnp.float32) - half) - half
    high = operator.astype(jnp.bfloat16)
    high_ref[...] = high
    low_ref[...] = (operator - high.astype(jnp.float32)).astype(jnp.bfloat16)
    for step in range(ITERS):
        summed = jnp.dot(
            high_ref[...], x_ref[...], preferred_element_type=jnp.float32
        ) + jnp.dot(low_ref[...], x_ref[...], preferred_element_type=jnp.float32)
        scale = jnp.sqrt(jnp.sum(summed * summed, 0, keepdims=True) / SEP_ROWS + epsilon)
        norms_ref[0, pl.ds(step, 1), :] = scale
        normed = (summed / scale).astype(jnp.bfloat16)
        if step < ITERS - 1:
            x_ref[...] = jnp.dot(
                normed, turns_ref[step], preferred_element_type=jnp.float32
            ).astype(jnp.bfloat16)
        else:
            x_ref[...] = normed
            rows = x_ref[pl.ds(pl.multiple_of(16 * device, STRIP), STRIP), :]
            out_ref[0] = jnp.dot(
                rows, turns_ref[step], preferred_element_type=jnp.float32
            ).astype(jnp.bfloat16)


def iterate(place, own, other, turns):
    return pl.pallas_call(
        iterate_kernel,
        in_specs=[SMEM, VMEM, VMEM, VMEM],
        out_specs=[VMEM, VMEM],
        out_shape=[
            jax.ShapeDtypeStruct((1, STRIP, COLS), jnp.bfloat16),
            jax.ShapeDtypeStruct((1, ITERS, COLS), jnp.float32),
        ],
        scratch_shapes=[
            pltpu.VMEM((SEP_ROWS, SEP_ROWS), jnp.bfloat16),
            pltpu.VMEM((SEP_ROWS, SEP_ROWS), jnp.float32),
            pltpu.VMEM((SEP_ROWS, SEP_ROWS), jnp.bfloat16),
            pltpu.VMEM((SEP_ROWS, SEP_ROWS), jnp.bfloat16),
            pltpu.VMEM((SEP_ROWS, COLS), jnp.bfloat16),
        ],
        name="iterate",
    )(place, own, other, turns)


SWAP = [(0, 1), (1, 0)]

def per_device(
    modes, coupling, eigenvalues, separator_of, row_offset, stiffness, start_block, rotations
):
    core = lax.axis_index("mode").astype(jnp.int32)
    device = lax.axis_index(("leaf", "mode")).astype(jnp.int32)
    other_eigen = lax.ppermute(eigenvalues, "mode", SWAP)
    eigen = jnp.where(
        core == 0,
        jnp.concatenate([eigenvalues, other_eigen], 1),
        jnp.concatenate([other_eigen, eigenvalues], 1),
    )
    own = jnp.einsum("ldw,ldm->lwm", coupling, modes, preferred_element_type=jnp.float32)
    other = lax.ppermute(own, "mode", SWAP)
    sep = lax.axis_index("sep").astype(jnp.int32)
    pieces = gram(separator_of[:, 0], row_offset, core[None], own, other, eigen)
    got = lax.all_to_all(pieces, "leaf", split_axis=0, concat_axis=0, tiled=True)
    plane = jnp.sum(got.astype(jnp.float32), 0).astype(jnp.bfloat16)
    rest = jnp.broadcast_to(plane[16:, None], (2, 4, STRIP, 128)).reshape(NSEP, 1, STRIP, 128)
    routed = jnp.concatenate([plane[:16].reshape(NSEP, 2, STRIP, 128), rest], 1)
    got = lax.all_to_all(routed, "sep", split_axis=0, concat_axis=0, tiled=True)
    window = jnp.sum(got.astype(jnp.float32), 0)
    high = window.astype(jnp.bfloat16)
    low = (window[0] - high[0].astype(jnp.float32)).astype(jnp.bfloat16)
    packed = jnp.concatenate(
        [stiffness[0].T, start_block[0], high[0], high[1], high[2], low], 1
    )
    mine = lax.all_to_all(
        jnp.broadcast_to(packed[None], (PLANE, *packed.shape)),
        "leaf",
        split_axis=0,
        concat_axis=0,
        tiled=True,
    )
    theirs = lax.ppermute(mine, "mode", SWAP)
    return tuple(iterate(jnp.stack([core, device, sep]), mine, theirs, rotations[0]))


def solution(mesh):
    in_specs = (
        P(("leaf", "sep"), "mode", None),
        P(("leaf", "sep"), "mode", None),
        P(("leaf", "sep"), "mode"),
        P(("leaf", "sep"), None),
        P(("leaf", "sep")),
        P("sep", None, ("leaf", "mode")),
        P("sep", ("leaf", "mode"), None),
        P("sep", None, None, None),
    )
    out_specs = (P("sep", ("leaf", "mode"), None), P("sep", None, None))
    return jax.shard_map(
        per_device, mesh=mesh, in_specs=in_specs, out_specs=out_specs, check_vma=False
    )
```

```python
import functools

import jax
import jax.numpy as jnp
from jax import lax
from jax.experimental import pallas as pl
from jax.experimental.pallas import tpu as pltpu
from jax.sharding import PartitionSpec as P

SEP_ROWS = 512
IFACE = 256
MODES = 256
COLS = 256
NSEP = 8
LEAF_DEV = 8
PLANE = 16
TILES = 18
STRIP = 16
ITERS = 2
epsilon = 1e-06


def gram_kernel(
    target_ref, offset_ref, core_ref, own_ref, other_ref, eigen_ref, other_eigen_ref, out_ref, pad_ref
):
    core = core_ref[0]
    row = lax.broadcasted_iota(jnp.int32, (SEP_ROWS, IFACE), 0)
    column = lax.broadcasted_iota(jnp.int32, (SEP_ROWS, IFACE), 1)
    distance = row - column
    pad_ref[LEAF_DEV] = jnp.zeros((SEP_ROWS, MODES), jnp.bfloat16)
    mine, theirs = eigen_ref[...], other_eigen_ref[...]
    eigen = jnp.concatenate(
        [jnp.where(core == 0, mine, theirs), jnp.where(core == 0, theirs, mine)], axis=1
    )
    inverses = 1.0 / jnp.sqrt(eigen)
    for leaf in range(LEAF_DEV):
        inverse = inverses[leaf : leaf + 1, :]
        product = own_ref[leaf].astype(jnp.float32) + other_ref[leaf].astype(jnp.float32)
        scaled = (product * inverse).astype(jnp.bfloat16)
        placing = (distance == offset_ref[leaf]).astype(jnp.bfloat16)
        pad_ref[leaf] = jnp.dot(placing, scaled, preferred_element_type=jnp.float32).astype(
            jnp.bfloat16
        )
    starts = [pl.multiple_of(32 * g + 16 * core, STRIP) for g in range(PLANE)]
    for s in range(NSEP):
        slots = [jnp.int32(LEAF_DEV), jnp.int32(LEAF_DEV)]
        for leaf in range(LEAF_DEV):
            hit = target_ref[leaf] == s
            later = hit & (slots[0] < LEAF_DEV)
            slots[1] = jnp.where(later, leaf, slots[1])
            slots[0] = jnp.where(hit & jnp.logical_not(later), leaf, slots[0])
        total = None
        for slot in slots:
            rows = jnp.concatenate([pad_ref[slot, pl.ds(x, STRIP), :] for x in starts], axis=0)
            product = lax.dot_general(
                rows, pad_ref[slot], (((1,), (1,)), ((), ())), preferred_element_type=jnp.float32
            )
            total = product if total is None else total + product
        lane = 32 * (s % 4)
        for g in range(PLANE):
            strip = total[g * STRIP : (g + 1) * STRIP, :]
            window = jnp.roll(strip, -32 * g, axis=1) if g else strip
            out_ref[g, 2 * s] = window[:, :128].astype(jnp.bfloat16)
            out_ref[g, 2 * s + 1] = window[:, 128:256].astype(jnp.bfloat16)
            rest = window[:, 256:384]
            rest = jnp.roll(rest, lane, axis=1) if lane else rest
            out_ref[g, 16 + s // 4, :, lane : lane + 32] = rest[:, lane : lane + 32].astype(
                jnp.bfloat16
            )


def in_vmem(x):
    return pltpu.with_memory_space_constraint(x, pltpu.VMEM)


VMEM = pl.BlockSpec(memory_space=pltpu.VMEM)
SMEM = pl.BlockSpec(memory_space=pltpu.SMEM)


def gram(target, offset, core, *arrays):
    return pl.pallas_call(
        gram_kernel,
        in_specs=[SMEM, SMEM, SMEM, VMEM, VMEM, VMEM, VMEM],
        out_specs=VMEM,
        out_shape=pltpu.VMEM((PLANE, TILES, STRIP, 128), jnp.bfloat16),
        scratch_shapes=[pltpu.VMEM((LEAF_DEV + 1, SEP_ROWS, MODES), jnp.bfloat16)],
        name="gram",
    )(target, offset, core, *[in_vmem(x) for x in arrays])


def iterate_kernel(
    place_ref, own_ref, other_ref, turns_ref, out_ref, norms_ref, kt_ref, m_ref, high_ref, low_ref, x_ref
):
    core, device, sep = place_ref[0], place_ref[1], place_ref[2]
    lane = lax.broadcasted_iota(jnp.int32, (STRIP, 128), 1)
    halved = jnp.where(lane < 32, 0.5, 1.0)
    rest_weight = jnp.where(lane < 32, 0.5, 0.0)
    back = (128 - 32 * (sep & 3)) & 127
    for ref, offset in ((own_ref, 16 * core), (other_ref, 16 * (1 - core))):
        for g in range(PLANE):
            rows = pl.ds(pl.multiple_of(32 * g + offset, STRIP), STRIP)
            kt_ref[rows, :] = ref[g, :, :512]
            x_ref[rows, :] = ref[g, :, 512:768]
            first = ref[g, :, 768:896].astype(jnp.float32) + ref[g, :, 1152:1280].astype(jnp.float32)
            second = ref[g, :, 896:1024].astype(jnp.float32)
            rest = pltpu.roll(ref[g, :, 1024:1152].astype(jnp.float32), back, axis=1)
            window = jnp.concatenate(
                [first * halved, second, rest * rest_weight, jnp.zeros_like(second)], axis=1
            )
            m_ref[rows, :] = jnp.roll(window, 32 * g, axis=1) if g else window
    half = m_ref[...]
    operator = jnp.transpose(kt_ref[...].astype(jnp.float32) - half) - half
    high = operator.astype(jnp.bfloat16)
    high_ref[...] = high
    low_ref[...] = (operator - high.astype(jnp.float32)).astype(jnp.bfloat16)
    for step in range(ITERS):
        summed = jnp.dot(
            high_ref[...], x_ref[...], preferred_element_type=jnp.float32
        ) + jnp.dot(low_ref[...], x_ref[...], preferred_element_type=jnp.float32)
        scale = jnp.sqrt(jnp.sum(summed * summed, 0, keepdims=True) / SEP_ROWS + epsilon)
        norms_ref[0, pl.ds(step, 1), :] = scale
        normed = (summed / scale).astype(jnp.bfloat16)
        if step < ITERS - 1:
            x_ref[...] = jnp.dot(
                normed, turns_ref[step], preferred_element_type=jnp.float32
            ).astype(jnp.bfloat16)
        else:
            x_ref[...] = normed
            rows = x_ref[pl.ds(pl.multiple_of(16 * device, STRIP), STRIP), :]
            out_ref[0] = jnp.dot(
                rows, turns_ref[step], preferred_element_type=jnp.float32
            ).astype(jnp.bfloat16)


def iterate(place, own, other, turns):
    return pl.pallas_call(
        iterate_kernel,
        in_specs=[SMEM, VMEM, VMEM, VMEM],
        out_specs=[VMEM, VMEM],
        out_shape=[
            jax.ShapeDtypeStruct((1, STRIP, COLS), jnp.bfloat16),
            jax.ShapeDtypeStruct((1, ITERS, COLS), jnp.float32),
        ],
        scratch_shapes=[
            pltpu.VMEM((SEP_ROWS, SEP_ROWS), jnp.bfloat16),
            pltpu.VMEM((SEP_ROWS, SEP_ROWS), jnp.float32),
            pltpu.VMEM((SEP_ROWS, SEP_ROWS), jnp.bfloat16),
            pltpu.VMEM((SEP_ROWS, SEP_ROWS), jnp.bfloat16),
            pltpu.VMEM((SEP_ROWS, COLS), jnp.bfloat16),
        ],
        name="iterate",
    )(place, in_vmem(own), in_vmem(other), turns)


SWAP = [(0, 1), (1, 0)]

def per_device(
    modes, coupling, eigenvalues, separator_of, row_offset, stiffness, start_block, rotations
):
    core = lax.axis_index("mode").astype(jnp.int32)
    device = lax.axis_index(("leaf", "mode")).astype(jnp.int32)
    other_eigen = lax.ppermute(eigenvalues, "mode", SWAP)
    own = jnp.einsum("ldw,ldm->lwm", coupling, modes, preferred_element_type=jnp.float32).astype(
        jnp.bfloat16
    )
    other = lax.ppermute(own, "mode", SWAP)
    sep = lax.axis_index("sep").astype(jnp.int32)
    pieces = gram(separator_of[:, 0], row_offset, core[None], own, other, eigenvalues, other_eigen)
    got = lax.all_to_all(pieces, "leaf", split_axis=0, concat_axis=0, tiled=True)
    plane = jnp.sum(got.astype(jnp.float32), 0).astype(jnp.bfloat16)
    rest = jnp.broadcast_to(plane[16:, None], (2, 4, STRIP, 128)).reshape(NSEP, 1, STRIP, 128)
    routed = jnp.concatenate([plane[:16].reshape(NSEP, 2, STRIP, 128), rest], 1)
    got = lax.all_to_all(routed, "sep", split_axis=0, concat_axis=0, tiled=True)
    window = jnp.sum(got.astype(jnp.float32), 0)
    high = window.astype(jnp.bfloat16)
    low = (window[0] - high[0].astype(jnp.float32)).astype(jnp.bfloat16)
    packed = jnp.concatenate(
        [stiffness[0].T, start_block[0], high[0], high[1], high[2], low], 1
    )
    mine = lax.all_to_all(
        jnp.broadcast_to(packed[None], (PLANE, *packed.shape)),
        "leaf",
        split_axis=0,
        concat_axis=0,
        tiled=True,
    )
    theirs = lax.ppermute(mine, "mode", SWAP)
    return tuple(iterate(jnp.stack([core, device, sep]), mine, theirs, rotations[0]))


def solution(mesh):
    in_specs = (
        P(("leaf", "sep"), "mode", None),
        P(("leaf", "sep"), "mode", None),
        P(("leaf", "sep"), "mode"),
        P(("leaf", "sep"), None),
        P(("leaf", "sep")),
        P("sep", None, ("leaf", "mode")),
        P("sep", ("leaf", "mode"), None),
        P("sep", None, None, None),
    )
    out_specs = (P("sep", ("leaf", "mode"), None), P("sep", None, None))
    return jax.shard_map(
        per_device, mesh=mesh, in_specs=in_specs, out_specs=out_specs, check_vma=False
    )
```

```python
import functools

import jax
import jax.numpy as jnp
from jax import lax
from jax.experimental import pallas as pl
from jax.experimental.pallas import tpu as pltpu
from jax.sharding import PartitionSpec as P

SEP_ROWS = 512
IFACE = 256
MODES = 256
COLS = 256
NSEP = 8
LEAF_DEV = 8
PLANE = 16
TILES = 18
STRIP = 16
ITERS = 2
epsilon = 1e-06


def gram_kernel(
    target_ref, offset_ref, core_ref, own_ref, other_ref, eigen_ref, other_eigen_ref, out_ref, window_ref, *pad_refs
):
    core = core_ref[0]
    reach = IFACE + STRIP
    row = lax.broadcasted_iota(jnp.int32, (reach, IFACE), 0)
    column = lax.broadcasted_iota(jnp.int32, (reach, IFACE), 1)
    distance = row - column
    mine, theirs = eigen_ref[...], other_eigen_ref[...]
    eigen = jnp.concatenate(
        [jnp.where(core == 0, mine, theirs), jnp.where(core == 0, theirs, mine)], axis=1
    )
    inverses = 1.0 / jnp.sqrt(eigen)
    starts = [pl.multiple_of(32 * g + 16 * core, STRIP) for g in range(PLANE)]
    window_ref[LEAF_DEV] = jnp.zeros((PLANE, STRIP, 384), jnp.float32)
    for leaf in range(LEAF_DEV):
        product = own_ref[leaf].astype(jnp.float32) + other_ref[leaf].astype(jnp.float32)
        scaled = (product * inverses[leaf : leaf + 1, :]).astype(jnp.bfloat16)
        offset = offset_ref[leaf]
        aligned = pl.multiple_of((offset >> 4) << 4, STRIP)
        placing = (distance == (offset & 15)).astype(jnp.bfloat16)
        pad_ref = pad_refs[leaf]
        pad_ref[...] = jnp.zeros_like(pad_ref)
        pad_ref[pl.ds(aligned, reach), :] = jnp.dot(
            placing, scaled, preferred_element_type=jnp.float32
        ).astype(jnp.bfloat16)
    for leaf in range(LEAF_DEV):
        pad_ref = pad_refs[leaf]
        rows = jnp.concatenate([pad_ref[pl.ds(x, STRIP), :] for x in starts], axis=0)
        total = lax.dot_general(
            rows,
            pad_ref[:SEP_ROWS, :],
            (((1,), (1,)), ((), ())),
            preferred_element_type=jnp.float32,
        )
        for g in range(PLANE):
            strip = total[g * STRIP : (g + 1) * STRIP, :]
            window_ref[leaf, g] = (pltpu.roll(strip, SEP_ROWS - 32 * g, axis=1) if g else strip)[:, :384]
    for s in range(NSEP):
        slots = [jnp.int32(LEAF_DEV), jnp.int32(LEAF_DEV)]
        for leaf in range(LEAF_DEV):
            hit = target_ref[leaf] == s
            later = hit & (slots[0] < LEAF_DEV)
            slots[1] = jnp.where(later, leaf, slots[1])
            slots[0] = jnp.where(hit & jnp.logical_not(later), leaf, slots[0])
        lane = 32 * (s % 4)
        for g in range(PLANE):
            window = window_ref[slots[0], g] + window_ref[slots[1], g]
            out_ref[g, 2 * s] = window[:, :128].astype(jnp.bfloat16)
            out_ref[g, 2 * s + 1] = window[:, 128:256].astype(jnp.bfloat16)
            rest = window[:, 256:384]
            rest = pltpu.roll(rest, lane, axis=1) if lane else rest
            out_ref[g, 16 + s // 4, :, lane : lane + 32] = rest[:, lane : lane + 32].astype(
                jnp.bfloat16
            )


def in_vmem(x):
    return pltpu.with_memory_space_constraint(x, pltpu.VMEM)


VMEM = pl.BlockSpec(memory_space=pltpu.VMEM)
SMEM = pl.BlockSpec(memory_space=pltpu.SMEM)


def gram(target, offset, core, *arrays):
    return pl.pallas_call(
        gram_kernel,
        in_specs=[SMEM, SMEM, SMEM, VMEM, VMEM, VMEM, VMEM],
        out_specs=VMEM,
        out_shape=pltpu.VMEM((PLANE, TILES, STRIP, 128), jnp.bfloat16),
        scratch_shapes=[
            pltpu.VMEM((LEAF_DEV + 1, PLANE, STRIP, 384), jnp.float32),
            *[pltpu.VMEM((SEP_ROWS + STRIP, MODES), jnp.bfloat16)] * LEAF_DEV,
        ],
        compiler_params=pltpu.CompilerParams(vmem_limit_bytes=24 << 20),
        name="gram",
    )(target, offset, core, *[in_vmem(x) for x in arrays])


def route_kernel(got_ref, out_ref):
    def total(tile):
        parts = [got_ref[k, tile].astype(jnp.float32) for k in range(PLANE)]
        while len(parts) > 1:
            parts = [a + b for a, b in zip(parts[::2], parts[1::2])]
        return parts[0].astype(jnp.bfloat16)

    for s in range(NSEP):
        out_ref[s, 0] = total(2 * s)
        out_ref[s, 1] = total(2 * s + 1)
    for k in range(2):
        rest = total(16 + k)
        for s in range(4 * k, 4 * k + 4):
            out_ref[s, 2] = rest


def route(got):
    return pl.pallas_call(
        route_kernel,
        in_specs=[VMEM],
        out_specs=VMEM,
        out_shape=pltpu.VMEM((NSEP, 3, STRIP, 128), jnp.bfloat16),
        compiler_params=pltpu.CompilerParams(vmem_limit_bytes=8 << 20),
        name="route",
    )(in_vmem(got))


def iterate_kernel(
    place_ref, own_ref, other_ref, turns_ref, out_ref, norms_ref, kt_ref, m_ref, high_ref, x_ref
):
    core, device, sep = place_ref[0], place_ref[1], place_ref[2]
    lane = lax.broadcasted_iota(jnp.int32, (STRIP, 128), 1)
    halved = jnp.where(lane < 32, 0.5, 1.0)
    rest_weight = jnp.where(lane < 32, 0.5, 0.0)
    back = (128 - 32 * (sep & 3)) & 127
    for ref, offset in ((own_ref, 16 * core), (other_ref, 16 * (1 - core))):
        for g in range(PLANE):
            rows = pl.ds(pl.multiple_of(32 * g + offset, STRIP), STRIP)
            kt_ref[rows, :] = ref[g, :, :512]
            x_ref[rows, :] = ref[g, :, 512:768]
            rest = pltpu.roll(ref[g, :, 1024:1152].astype(jnp.float32), back, axis=1)
            low = jnp.where(lane < 32, pltpu.roll(rest, 96, axis=1), 0.0)
            first = ref[g, :, 768:896].astype(jnp.float32) + low
            second = ref[g, :, 896:1024].astype(jnp.float32)
            window = jnp.concatenate(
                [first * halved, second, rest * rest_weight, jnp.zeros_like(second)], axis=1
            )
            m_ref[rows, :] = pltpu.roll(window, 32 * g, axis=1) if g else window
    half = m_ref[...]
    operator = jnp.transpose(kt_ref[...].astype(jnp.float32) - half) - half
    high = operator.astype(jnp.bfloat16)
    high_ref[...] = high
    error = operator - high.astype(jnp.float32)
    across = lax.broadcasted_iota(jnp.int32, (128, 128), 0)
    along = lax.broadcasted_iota(jnp.int32, (128, 128), 1)
    low = jnp.concatenate(
        [
            jnp.sum(jnp.where(across == along, error[k : k + 128, k : k + 128], 0.0), 1, keepdims=True)
            for k in range(0, SEP_ROWS, 128)
        ],
        axis=0,
    )
    for step in range(ITERS):
        block = x_ref[...]
        summed = jnp.dot(high_ref[...], block, preferred_element_type=jnp.float32)
        summed = summed + low * block.astype(jnp.float32)
        scale = jnp.sqrt(jnp.sum(summed * summed, 0, keepdims=True) / SEP_ROWS + epsilon)
        norms_ref[0, pl.ds(step, 1), :] = scale
        normed = (summed / scale).astype(jnp.bfloat16)
        if step < ITERS - 1:
            x_ref[...] = jnp.dot(
                normed, turns_ref[step], preferred_element_type=jnp.float32
            ).astype(jnp.bfloat16)
        else:
            x_ref[...] = normed
            rows = x_ref[pl.ds(pl.multiple_of(16 * device, STRIP), STRIP), :]
            out_ref[0] = jnp.dot(
                rows, turns_ref[step], preferred_element_type=jnp.float32
            ).astype(jnp.bfloat16)


def iterate(place, own, other, turns):
    return pl.pallas_call(
        iterate_kernel,
        in_specs=[SMEM, VMEM, VMEM, VMEM],
        out_specs=[VMEM, VMEM],
        out_shape=[
            jax.ShapeDtypeStruct((1, STRIP, COLS), jnp.bfloat16),
            jax.ShapeDtypeStruct((1, ITERS, COLS), jnp.float32),
        ],
        scratch_shapes=[
            pltpu.VMEM((SEP_ROWS, SEP_ROWS), jnp.bfloat16),
            pltpu.VMEM((SEP_ROWS, SEP_ROWS), jnp.float32),
            pltpu.VMEM((SEP_ROWS, SEP_ROWS), jnp.bfloat16),
            pltpu.VMEM((SEP_ROWS, COLS), jnp.bfloat16),
        ],
        compiler_params=pltpu.CompilerParams(vmem_limit_bytes=16 << 20),
        name="iterate",
    )(place, in_vmem(own), in_vmem(other), in_vmem(turns))


SWAP = [(0, 1), (1, 0)]

def per_device(
    modes, coupling, eigenvalues, separator_of, row_offset, stiffness, start_block, rotations
):
    core = lax.axis_index("mode").astype(jnp.int32)
    device = lax.axis_index(("leaf", "mode")).astype(jnp.int32)
    other_eigen = lax.ppermute(eigenvalues, "mode", SWAP)
    own = jnp.einsum("ldw,ldm->lwm", coupling, modes, preferred_element_type=jnp.float32).astype(
        jnp.bfloat16
    )
    other = lax.ppermute(own, "mode", SWAP)
    sep = lax.axis_index("sep").astype(jnp.int32)
    pieces = gram(separator_of[:, 0], row_offset, core[None], own, other, eigenvalues, other_eigen)
    got = lax.all_to_all(pieces, "leaf", split_axis=0, concat_axis=0, tiled=True)
    got = lax.all_to_all(route(got), "sep", split_axis=0, concat_axis=0, tiled=True)
    window = jnp.sum(got.astype(jnp.float32), 0)
    high = window.astype(jnp.bfloat16)
    low = (window[0] - high[0].astype(jnp.float32)).astype(jnp.bfloat16)
    group = lax.broadcasted_iota(jnp.int32, (STRIP, 128), 1) >> 5
    rest = jnp.where(group == (sep & 3), high[2], jnp.concatenate([low[:, :32]] * 4, 1))
    packed = jnp.concatenate([stiffness[0].T, start_block[0], high[0], high[1], rest], 1)
    mine = lax.all_to_all(
        jnp.broadcast_to(packed[None], (PLANE, *packed.shape)),
        "leaf",
        split_axis=0,
        concat_axis=0,
        tiled=True,
    )
    theirs = lax.ppermute(mine, "mode", SWAP)
    return tuple(iterate(jnp.stack([core, device, sep]), mine, theirs, rotations[0]))


def solution(mesh):
    in_specs = (
        P(("leaf", "sep"), "mode", None),
        P(("leaf", "sep"), "mode", None),
        P(("leaf", "sep"), "mode"),
        P(("leaf", "sep"), None),
        P(("leaf", "sep")),
        P("sep", None, ("leaf", "mode")),
        P("sep", ("leaf", "mode"), None),
        P("sep", None, None, None),
    )
    out_specs = (P("sep", ("leaf", "mode"), None), P("sep", None, None))
    return jax.shard_map(
        per_device, mesh=mesh, in_specs=in_specs, out_specs=out_specs, check_vma=False
    )
```

```python
import functools

import jax
import jax.numpy as jnp
from jax import lax
from jax.experimental import pallas as pl
from jax.experimental.pallas import tpu as pltpu
from jax.sharding import PartitionSpec as P

SEP_ROWS = 512
IFACE = 256
MODES = 256
COLS = 256
NSEP = 8
LEAF_DEV = 8
PLANE = 16
SIDE = 4
GROUPS = 8
TILES = 18
STRIP = 16
ITERS = 2
epsilon = 1e-06


def place_of(d, e, place_ref):
    one = (place_ref[1] + d) & (SIDE - 1)
    two = (place_ref[2] + e) & (SIDE - 1)
    return jnp.where(place_ref[0] == 0, two * SIDE + one, one * SIDE + two)


def gram_kernel(
    target_ref, offset_ref, place_ref, own_ref, other_ref, eigen_ref, other_eigen_ref, *refs
):
    out_refs, window_ref, pad_refs = refs[:SIDE], refs[SIDE], refs[SIDE + 1 :]
    core = place_ref[0]
    reach = IFACE + STRIP
    row = lax.broadcasted_iota(jnp.int32, (reach, IFACE), 0)
    column = lax.broadcasted_iota(jnp.int32, (reach, IFACE), 1)
    distance = row - column
    mine, theirs = eigen_ref[...], other_eigen_ref[...]
    eigen = jnp.concatenate(
        [jnp.where(core == 0, mine, theirs), jnp.where(core == 0, theirs, mine)], axis=1
    )
    inverses = 1.0 / jnp.sqrt(eigen)
    starts = [pl.multiple_of(32 * g + 16 * core, STRIP) for g in range(PLANE)]
    window_ref[LEAF_DEV] = jnp.zeros((PLANE, STRIP, 384), jnp.float32)
    for leaf in range(LEAF_DEV):
        product = own_ref[leaf].astype(jnp.float32) + other_ref[leaf].astype(jnp.float32)
        scaled = (product * inverses[leaf : leaf + 1, :]).astype(jnp.bfloat16)
        offset = offset_ref[leaf]
        aligned = pl.multiple_of((offset >> 4) << 4, STRIP)
        placing = (distance == (offset & 15)).astype(jnp.bfloat16)
        pad_ref = pad_refs[leaf]
        pad_ref[...] = jnp.zeros_like(pad_ref)
        pad_ref[pl.ds(aligned, reach), :] = jnp.dot(
            placing, scaled, preferred_element_type=jnp.float32
        ).astype(jnp.bfloat16)
    for leaf in range(LEAF_DEV):
        pad_ref = pad_refs[leaf]
        rows = jnp.concatenate([pad_ref[pl.ds(x, STRIP), :] for x in starts], axis=0)
        total = lax.dot_general(
            rows,
            pad_ref[:SEP_ROWS, :],
            (((1,), (1,)), ((), ())),
            preferred_element_type=jnp.float32,
        )
        for g in range(PLANE):
            strip = total[g * STRIP : (g + 1) * STRIP, :]
            window_ref[leaf, g] = (pltpu.roll(strip, SEP_ROWS - 32 * g, axis=1) if g else strip)[:, :384]
    places = [place_of(k // SIDE, k % SIDE, place_ref) for k in range(PLANE)]
    for s in range(NSEP):
        slots = [jnp.int32(LEAF_DEV), jnp.int32(LEAF_DEV)]
        for leaf in range(LEAF_DEV):
            hit = target_ref[leaf] == s
            later = hit & (slots[0] < LEAF_DEV)
            slots[1] = jnp.where(later, leaf, slots[1])
            slots[0] = jnp.where(hit & jnp.logical_not(later), leaf, slots[0])
        lane = 32 * (s % 4)
        for k in range(PLANE):
            g = places[k]
            out_ref, e = out_refs[k // SIDE], k % SIDE
            window = window_ref[slots[0], g] + window_ref[slots[1], g]
            out_ref[e, 2 * s] = window[:, :128].astype(jnp.bfloat16)
            out_ref[e, 2 * s + 1] = window[:, 128:256].astype(jnp.bfloat16)
            rest = window[:, 256:384]
            rest = pltpu.roll(rest, lane, axis=1) if lane else rest
            out_ref[e, 16 + s // 4, :, lane : lane + 32] = rest[:, lane : lane + 32].astype(
                jnp.bfloat16
            )


def in_vmem(x):
    return pltpu.with_memory_space_constraint(x, pltpu.VMEM)


VMEM = pl.BlockSpec(memory_space=pltpu.VMEM)
SMEM = pl.BlockSpec(memory_space=pltpu.SMEM)


def gram(target, offset, place, *arrays):
    return pl.pallas_call(
        gram_kernel,
        in_specs=[SMEM, SMEM, SMEM, VMEM, VMEM, VMEM, VMEM],
        out_specs=[VMEM] * SIDE,
        out_shape=[jax.ShapeDtypeStruct((SIDE, TILES, STRIP, 128), jnp.bfloat16)] * SIDE,
        scratch_shapes=[
            pltpu.VMEM((LEAF_DEV + 1, PLANE, STRIP, 384), jnp.float32),
            *[pltpu.VMEM((SEP_ROWS + STRIP, MODES), jnp.bfloat16)] * LEAF_DEV,
        ],
        compiler_params=pltpu.CompilerParams(vmem_limit_bytes=24 << 20),
        name="gram",
    )(target, offset, place, *[in_vmem(x) for x in arrays])


def total(refs, *where):
    return sum(ref[where].astype(jnp.float32) for ref in refs).astype(jnp.bfloat16)


def split_kernel(*refs):
    sources, outs = refs[:SIDE], refs[SIDE:]
    for e in range(SIDE):
        for tile in range(TILES):
            outs[e][tile] = total(sources, e, tile)


def route_kernel(*refs):
    sources, out_ref = refs[:SIDE], refs[SIDE]
    for s in range(NSEP):
        out_ref[s, 0] = total(sources, 2 * s)
        out_ref[s, 1] = total(sources, 2 * s + 1)
    for k in range(2):
        rest = total(sources, 16 + k)
        for s in range(4 * k, 4 * k + 4):
            out_ref[s, 2] = rest


def combine(kernel, pieces, shapes):
    return pl.pallas_call(
        kernel,
        in_specs=[VMEM] * SIDE,
        out_specs=[VMEM] * len(shapes),
        out_shape=[jax.ShapeDtypeStruct(shape, jnp.bfloat16) for shape in shapes],
        compiler_params=pltpu.CompilerParams(vmem_limit_bytes=8 << 20),
        name=kernel.__name__,
    )(*[in_vmem(piece) for piece in pieces])


def iterate_kernel(
    place_ref, own_ref, other_ref, turns_ref, out_ref, norms_ref, kt_ref, m_ref, high_ref, x_ref
):
    core, device, sep = place_ref[0], place_ref[1], place_ref[2]
    lane = lax.broadcasted_iota(jnp.int32, (STRIP, 128), 1)
    halved = jnp.where(lane < 32, 0.5, 1.0)
    rest_weight = jnp.where(lane < 32, 0.5, 0.0)
    back = (128 - 32 * (sep & 3)) & 127
    for ref, offset in ((own_ref, 16 * core), (other_ref, 16 * (1 - core))):
        for g in range(PLANE):
            rows = pl.ds(pl.multiple_of(32 * g + offset, STRIP), STRIP)
            kt_ref[rows, :] = ref[g, :, :512]
            x_ref[rows, :] = ref[g, :, 512:768]
            rest = pltpu.roll(ref[g, :, 1024:1152].astype(jnp.float32), back, axis=1)
            low = jnp.where(lane < 32, pltpu.roll(rest, 96, axis=1), 0.0)
            first = ref[g, :, 768:896].astype(jnp.float32) + low
            second = ref[g, :, 896:1024].astype(jnp.float32)
            window = jnp.concatenate(
                [first * halved, second, rest * rest_weight, jnp.zeros_like(second)], axis=1
            )
            m_ref[rows, :] = pltpu.roll(window, 32 * g, axis=1) if g else window
    half = m_ref[...]
    operator = jnp.transpose(kt_ref[...].astype(jnp.float32) - half) - half
    high = operator.astype(jnp.bfloat16)
    high_ref[...] = high
    error = operator - high.astype(jnp.float32)
    across = lax.broadcasted_iota(jnp.int32, (128, 128), 0)
    along = lax.broadcasted_iota(jnp.int32, (128, 128), 1)
    low = jnp.concatenate(
        [
            jnp.sum(jnp.where(across == along, error[k : k + 128, k : k + 128], 0.0), 1, keepdims=True)
            for k in range(0, SEP_ROWS, 128)
        ],
        axis=0,
    )
    for step in range(ITERS):
        block = x_ref[...]
        summed = jnp.dot(high_ref[...], block, preferred_element_type=jnp.float32)
        summed = summed + low * block.astype(jnp.float32)
        scale = jnp.sqrt(jnp.sum(summed * summed, 0, keepdims=True) / SEP_ROWS + epsilon)
        norms_ref[0, pl.ds(step, 1), :] = scale
        normed = (summed / scale).astype(jnp.bfloat16)
        if step < ITERS - 1:
            x_ref[...] = jnp.dot(
                normed, turns_ref[step], preferred_element_type=jnp.float32
            ).astype(jnp.bfloat16)
        else:
            x_ref[...] = normed
            rows = x_ref[pl.ds(pl.multiple_of(16 * device, STRIP), STRIP), :]
            out_ref[0] = jnp.dot(
                rows, turns_ref[step], preferred_element_type=jnp.float32
            ).astype(jnp.bfloat16)


def iterate(place, own, other, turns):
    return pl.pallas_call(
        iterate_kernel,
        in_specs=[SMEM, VMEM, VMEM, VMEM],
        out_specs=[VMEM, VMEM],
        out_shape=[
            jax.ShapeDtypeStruct((1, STRIP, COLS), jnp.bfloat16),
            jax.ShapeDtypeStruct((1, ITERS, COLS), jnp.float32),
        ],
        scratch_shapes=[
            pltpu.VMEM((SEP_ROWS, SEP_ROWS), jnp.bfloat16),
            pltpu.VMEM((SEP_ROWS, SEP_ROWS), jnp.float32),
            pltpu.VMEM((SEP_ROWS, SEP_ROWS), jnp.bfloat16),
            pltpu.VMEM((SEP_ROWS, COLS), jnp.bfloat16),
        ],
        compiler_params=pltpu.CompilerParams(vmem_limit_bytes=16 << 20),
        name="iterate",
    )(place, in_vmem(own), in_vmem(other), in_vmem(turns))


SWAP = [(0, 1), (1, 0)]
AXES = ("leaf", "sep", "mode")


def index_of(y, x, z, core):
    return ((y * SIDE + x) * GROUPS + z) * 2 + core


def plane_steps(step, stage):
    pairs = []
    for y in range(SIDE):
        for x in range(SIDE):
            for z in range(GROUPS):
                for core in range(2):
                    along_x = (core + stage) % 2 == 0
                    to = (y, (x + step) % SIDE) if along_x else ((y + step) % SIDE, x)
                    pairs.append((index_of(y, x, z, core), index_of(*to, z, core)))
    return pairs


def scatter_stage(pieces, stage):
    got = [lax.ppermute(pieces[d], AXES, plane_steps(d, stage)) for d in ORDER]
    return [pieces[0], *got]


ORDER = (1, 3, 2)

def per_device(
    modes, coupling, eigenvalues, separator_of, row_offset, stiffness, start_block, rotations
):
    core = lax.axis_index("mode").astype(jnp.int32)
    device = lax.axis_index(("leaf", "mode")).astype(jnp.int32)
    other_eigen = lax.ppermute(eigenvalues, "mode", SWAP)
    own = jnp.einsum("ldw,ldm->lwm", coupling, modes, preferred_element_type=jnp.float32).astype(
        jnp.bfloat16
    )
    other = lax.ppermute(own, "mode", SWAP)
    sep = lax.axis_index("sep").astype(jnp.int32)
    leaf = lax.axis_index("leaf").astype(jnp.int32)
    y, x = leaf >> 2, leaf & 3
    place = jnp.stack([core, jnp.where(core == 0, x, y), jnp.where(core == 0, y, x)])
    pieces = gram(separator_of[:, 0], row_offset, place, own, other, eigenvalues, other_eigen)
    piece = (TILES, STRIP, 128)
    pieces = combine(split_kernel, scatter_stage(pieces, 0), [piece] * SIDE)
    (routed,) = combine(route_kernel, scatter_stage(pieces, 1), [(NSEP, 3, STRIP, 128)])
    got = lax.all_to_all(routed, "sep", split_axis=0, concat_axis=0, tiled=True)
    window = jnp.sum(got.astype(jnp.float32), 0)
    high = window.astype(jnp.bfloat16)
    low = (window[0] - high[0].astype(jnp.float32)).astype(jnp.bfloat16)
    group = lax.broadcasted_iota(jnp.int32, (STRIP, 128), 1) >> 5
    rest = jnp.where(group == (sep & 3), high[2], jnp.concatenate([low[:, :32]] * 4, 1))
    packed = jnp.concatenate([stiffness[0].T, start_block[0], high[0], high[1], rest], 1)
    mine = lax.all_to_all(
        jnp.broadcast_to(packed[None], (PLANE, *packed.shape)),
        "leaf",
        split_axis=0,
        concat_axis=0,
        tiled=True,
    )
    theirs = lax.ppermute(mine, "mode", SWAP)
    return tuple(iterate(jnp.stack([core, device, sep]), mine, theirs, rotations[0]))


def solution(mesh):
    in_specs = (
        P(("leaf", "sep"), "mode", None),
        P(("leaf", "sep"), "mode", None),
        P(("leaf", "sep"), "mode"),
        P(("leaf", "sep"), None),
        P(("leaf", "sep")),
        P("sep", None, ("leaf", "mode")),
        P("sep", ("leaf", "mode"), None),
        P("sep", None, None, None),
    )
    out_specs = (P("sep", ("leaf", "mode"), None), P("sep", None, None))
    return jax.shard_map(
        per_device, mesh=mesh, in_specs=in_specs, out_specs=out_specs, check_vma=False
    )
```

```python
import functools

import jax
import jax.numpy as jnp
from jax import lax
from jax.experimental import pallas as pl
from jax.experimental.pallas import tpu as pltpu
from jax.sharding import PartitionSpec as P

SEP_ROWS = 512
IFACE = 256
MODES = 256
COLS = 256
NSEP = 8
LEAF_DEV = 8
PLANE = 16
SIDE = 4
GROUPS = 8
TILES = 18
STRIP = 16
ITERS = 2
epsilon = 1e-06


def place_of(d, e, place_ref):
    one = (place_ref[1] + d) & (SIDE - 1)
    two = (place_ref[2] + e) & (SIDE - 1)
    return jnp.where(place_ref[0] == 0, two * SIDE + one, one * SIDE + two)


def gram_kernel(
    target_ref, offset_ref, place_ref, own_ref, other_ref, eigen_ref, other_eigen_ref, *refs
):
    out_refs, window_ref, pad_refs = refs[:SIDE], refs[SIDE], refs[SIDE + 1 :]
    core = place_ref[0]
    reach = IFACE + STRIP
    row = lax.broadcasted_iota(jnp.int32, (reach, IFACE), 0)
    column = lax.broadcasted_iota(jnp.int32, (reach, IFACE), 1)
    distance = row - column
    mine, theirs = eigen_ref[...], other_eigen_ref[...]
    eigen = jnp.concatenate(
        [jnp.where(core == 0, mine, theirs), jnp.where(core == 0, theirs, mine)], axis=1
    )
    inverses = 1.0 / jnp.sqrt(eigen)
    starts = [pl.multiple_of(32 * g + 16 * core, STRIP) for g in range(PLANE)]
    window_ref[LEAF_DEV] = jnp.zeros((PLANE, STRIP, 384), jnp.float32)
    for leaf in range(LEAF_DEV):
        product = own_ref[leaf].astype(jnp.float32) + other_ref[leaf].astype(jnp.float32)
        scaled = (product * inverses[leaf : leaf + 1, :]).astype(jnp.bfloat16)
        offset = offset_ref[leaf]
        aligned = pl.multiple_of((offset >> 4) << 4, STRIP)
        placing = (distance == (offset & 15)).astype(jnp.bfloat16)
        pad_ref = pad_refs[leaf]
        pad_ref[...] = jnp.zeros_like(pad_ref)
        pad_ref[pl.ds(aligned, reach), :] = jnp.dot(
            placing, scaled, preferred_element_type=jnp.float32
        ).astype(jnp.bfloat16)
    for leaf in range(LEAF_DEV):
        pad_ref = pad_refs[leaf]
        rows = jnp.concatenate([pad_ref[pl.ds(x, STRIP), :] for x in starts], axis=0)
        total = lax.dot_general(
            rows,
            pad_ref[:SEP_ROWS, :],
            (((1,), (1,)), ((), ())),
            preferred_element_type=jnp.float32,
        )
        for g in range(PLANE):
            strip = total[g * STRIP : (g + 1) * STRIP, :]
            window_ref[leaf, g] = (pltpu.roll(strip, SEP_ROWS - 32 * g, axis=1) if g else strip)[:, :384]
    places = [place_of(k // SIDE, k % SIDE, place_ref) for k in range(PLANE)]
    for s in range(NSEP):
        slots = [jnp.int32(LEAF_DEV), jnp.int32(LEAF_DEV)]
        for leaf in range(LEAF_DEV):
            hit = target_ref[leaf] == s
            later = hit & (slots[0] < LEAF_DEV)
            slots[1] = jnp.where(later, leaf, slots[1])
            slots[0] = jnp.where(hit & jnp.logical_not(later), leaf, slots[0])
        lane = 32 * (s % 4)
        for k in range(PLANE):
            g = places[k]
            out_ref, e = out_refs[k // SIDE], k % SIDE
            window = window_ref[slots[0], g] + window_ref[slots[1], g]
            out_ref[e, 2 * s] = window[:, :128].astype(jnp.bfloat16)
            out_ref[e, 2 * s + 1] = window[:, 128:256].astype(jnp.bfloat16)
            rest = window[:, 256:384]
            rest = pltpu.roll(rest, lane, axis=1) if lane else rest
            out_ref[e, 16 + s // 4, :, lane : lane + 32] = rest[:, lane : lane + 32].astype(
                jnp.bfloat16
            )


def in_vmem(x):
    return pltpu.with_memory_space_constraint(x, pltpu.VMEM)


VMEM = pl.BlockSpec(memory_space=pltpu.VMEM)
SMEM = pl.BlockSpec(memory_space=pltpu.SMEM)


def gram(target, offset, place, *arrays):
    return pl.pallas_call(
        gram_kernel,
        in_specs=[SMEM, SMEM, SMEM, VMEM, VMEM, VMEM, VMEM],
        out_specs=[VMEM] * SIDE,
        out_shape=[jax.ShapeDtypeStruct((SIDE, TILES, STRIP, 128), jnp.bfloat16)] * SIDE,
        scratch_shapes=[
            pltpu.VMEM((LEAF_DEV + 1, PLANE, STRIP, 384), jnp.float32),
            *[pltpu.VMEM((SEP_ROWS + STRIP, MODES), jnp.bfloat16)] * LEAF_DEV,
        ],
        compiler_params=pltpu.CompilerParams(vmem_limit_bytes=24 << 20),
        name="gram",
    )(target, offset, place, *[in_vmem(x) for x in arrays])


def total(refs, *where):
    return sum(ref[where].astype(jnp.float32) for ref in refs).astype(jnp.bfloat16)


def split_kernel(*refs):
    sources, outs = refs[:SIDE], refs[SIDE:]
    for e in range(SIDE):
        for tile in range(TILES):
            outs[e][tile] = total(sources, e, tile)


def route_kernel(*refs):
    sources, out_ref = refs[:SIDE], refs[SIDE]
    for s in range(NSEP):
        out_ref[s, 0] = total(sources, 2 * s)
        out_ref[s, 1] = total(sources, 2 * s + 1)
    for k in range(2):
        rest = total(sources, 16 + k)
        for s in range(4 * k, 4 * k + 4):
            out_ref[s, 2] = rest


def combine(kernel, pieces, shapes):
    return pl.pallas_call(
        kernel,
        in_specs=[VMEM] * SIDE,
        out_specs=[VMEM] * len(shapes),
        out_shape=[jax.ShapeDtypeStruct(shape, jnp.bfloat16) for shape in shapes],
        compiler_params=pltpu.CompilerParams(vmem_limit_bytes=8 << 20),
        name=kernel.__name__,
    )(*[in_vmem(piece) for piece in pieces])


def iterate_kernel(
    place_ref, own_ref, other_ref, known_ref, known_other_ref, turns_ref, out_ref, norms_ref, kt_ref, m_ref, high_ref, x_ref
):
    core, device, sep = place_ref[0], place_ref[1], place_ref[2]
    leaf = device >> 1
    y, x = leaf >> 2, leaf & 3
    lane = lax.broadcasted_iota(jnp.int32, (STRIP, 128), 1)
    halved = jnp.where(lane < 32, 0.5, 1.0)
    rest_weight = jnp.where(lane < 32, 0.5, 0.0)
    back = (128 - 32 * (sep & 3)) & 127
    for ref, known, which in ((own_ref, known_ref, core), (other_ref, known_other_ref, 1 - core)):
        for e in range(SIDE):
            for d in range(SIDE):
                up = (y - jnp.where(which == 0, e, d)) & (SIDE - 1)
                over = (x - jnp.where(which == 0, d, e)) & (SIDE - 1)
                start = 32 * (up * SIDE + over) + 16 * which
                rows = pl.ds(pl.multiple_of(start, STRIP), STRIP)
                kt_ref[rows, :] = known[e, d, :, :SEP_ROWS]
                x_ref[rows, :] = known[e, d, :, SEP_ROWS:]
        for g in range(PLANE):
            rows = pl.ds(pl.multiple_of(32 * g + 16 * which, STRIP), STRIP)
            rest = pltpu.roll(ref[g, :, 256:384].astype(jnp.float32), back, axis=1)
            low = jnp.where(lane < 32, pltpu.roll(rest, 96, axis=1), 0.0)
            first = ref[g, :, :128].astype(jnp.float32) + low
            second = ref[g, :, 128:256].astype(jnp.float32)
            window = jnp.concatenate(
                [first * halved, second, rest * rest_weight, jnp.zeros_like(second)], axis=1
            )
            m_ref[rows, :] = pltpu.roll(window, 32 * g, axis=1) if g else window
    half = m_ref[...]
    operator = jnp.transpose(kt_ref[...].astype(jnp.float32) - half) - half
    high = operator.astype(jnp.bfloat16)
    high_ref[...] = high
    error = operator - high.astype(jnp.float32)
    across = lax.broadcasted_iota(jnp.int32, (128, 128), 0)
    along = lax.broadcasted_iota(jnp.int32, (128, 128), 1)
    low = jnp.concatenate(
        [
            jnp.sum(jnp.where(across == along, error[k : k + 128, k : k + 128], 0.0), 1, keepdims=True)
            for k in range(0, SEP_ROWS, 128)
        ],
        axis=0,
    )
    for step in range(ITERS):
        block = x_ref[...]
        summed = jnp.dot(high_ref[...], block, preferred_element_type=jnp.float32)
        summed = summed + low * block.astype(jnp.float32)
        scale = jnp.sqrt(jnp.sum(summed * summed, 0, keepdims=True) / SEP_ROWS + epsilon)
        norms_ref[0, pl.ds(step, 1), :] = scale
        normed = (summed / scale).astype(jnp.bfloat16)
        if step < ITERS - 1:
            x_ref[...] = jnp.dot(
                normed, turns_ref[step], preferred_element_type=jnp.float32
            ).astype(jnp.bfloat16)
        else:
            x_ref[...] = normed
            rows = x_ref[pl.ds(pl.multiple_of(16 * device, STRIP), STRIP), :]
            out_ref[0] = jnp.dot(
                rows, turns_ref[step], preferred_element_type=jnp.float32
            ).astype(jnp.bfloat16)


def iterate(place, *arrays):
    return pl.pallas_call(
        iterate_kernel,
        in_specs=[SMEM] + [VMEM] * len(arrays),
        out_specs=[VMEM, VMEM],
        out_shape=[
            jax.ShapeDtypeStruct((1, STRIP, COLS), jnp.bfloat16),
            jax.ShapeDtypeStruct((1, ITERS, COLS), jnp.float32),
        ],
        scratch_shapes=[
            pltpu.VMEM((SEP_ROWS, SEP_ROWS), jnp.bfloat16),
            pltpu.VMEM((SEP_ROWS, SEP_ROWS), jnp.float32),
            pltpu.VMEM((SEP_ROWS, SEP_ROWS), jnp.bfloat16),
            pltpu.VMEM((SEP_ROWS, COLS), jnp.bfloat16),
        ],
        compiler_params=pltpu.CompilerParams(vmem_limit_bytes=16 << 20),
        name="iterate",
    )(place, *[in_vmem(array) for array in arrays])


SWAP = [(0, 1), (1, 0)]
AXES = ("leaf", "sep", "mode")


def index_of(y, x, z, core):
    return ((y * SIDE + x) * GROUPS + z) * 2 + core


def plane_steps(step, stage):
    pairs = []
    for y in range(SIDE):
        for x in range(SIDE):
            for z in range(GROUPS):
                for core in range(2):
                    along_x = (core + stage) % 2 == 0
                    to = (y, (x + step) % SIDE) if along_x else ((y + step) % SIDE, x)
                    pairs.append((index_of(y, x, z, core), index_of(*to, z, core)))
    return pairs


def after(value, earlier):
    return lax.optimization_barrier((value, earlier))[0]


def gather_stage(value, stage):
    got = [lax.ppermute(value, AXES, plane_steps(d, stage)) for d in ORDER]
    return jnp.stack([value, got[0], got[2], got[1]])


def scatter_stage(pieces, stage):
    got = [lax.ppermute(pieces[d], AXES, plane_steps(d, stage)) for d in ORDER]
    return [pieces[0], *got]


ORDER = (1, 3, 2)

def per_device(
    modes, coupling, eigenvalues, separator_of, row_offset, stiffness, start_block, rotations
):
    core = lax.axis_index("mode").astype(jnp.int32)
    device = lax.axis_index(("leaf", "mode")).astype(jnp.int32)
    other_eigen = lax.ppermute(eigenvalues, "mode", SWAP)
    own = jnp.einsum("ldw,ldm->lwm", coupling, modes, preferred_element_type=jnp.float32).astype(
        jnp.bfloat16
    )
    other = lax.ppermute(own, "mode", SWAP)
    sep = lax.axis_index("sep").astype(jnp.int32)
    leaf = lax.axis_index("leaf").astype(jnp.int32)
    y, x = leaf >> 2, leaf & 3
    place = jnp.stack([core, jnp.where(core == 0, x, y), jnp.where(core == 0, y, x)])
    pieces = gram(separator_of[:, 0], row_offset, place, own, other, eigenvalues, other_eigen)
    piece = (TILES, STRIP, 128)
    known = jnp.concatenate([stiffness[0].T, start_block[0]], 1)
    near = gather_stage(after(known, pieces[0]), 0)
    pieces = combine(split_kernel, scatter_stage(pieces, 0), [piece] * SIDE)
    known = gather_stage(after(near, pieces[0]), 1)
    (routed,) = combine(route_kernel, scatter_stage(pieces, 1), [(NSEP, 3, STRIP, 128)])
    known_other = lax.ppermute(after(known, routed), "mode", SWAP)
    got = lax.all_to_all(routed, "sep", split_axis=0, concat_axis=0, tiled=True)
    window = jnp.sum(got.astype(jnp.float32), 0)
    high = window.astype(jnp.bfloat16)
    low = (window[0] - high[0].astype(jnp.float32)).astype(jnp.bfloat16)
    group = lax.broadcasted_iota(jnp.int32, (STRIP, 128), 1) >> 5
    rest = jnp.where(group == (sep & 3), high[2], jnp.concatenate([low[:, :32]] * 4, 1))
    packed = jnp.concatenate([high[0], high[1], rest], 1)
    mine = lax.all_to_all(
        jnp.broadcast_to(packed[None], (PLANE, *packed.shape)),
        "leaf",
        split_axis=0,
        concat_axis=0,
        tiled=True,
    )
    theirs = lax.ppermute(mine, "mode", SWAP)
    place = jnp.stack([core, device, sep])
    return tuple(iterate(place, mine, theirs, known, known_other, rotations[0]))


def solution(mesh):
    in_specs = (
        P(("leaf", "sep"), "mode", None),
        P(("leaf", "sep"), "mode", None),
        P(("leaf", "sep"), "mode"),
        P(("leaf", "sep"), None),
        P(("leaf", "sep")),
        P("sep", None, ("leaf", "mode")),
        P("sep", ("leaf", "mode"), None),
        P("sep", None, None, None),
    )
    out_specs = (P("sep", ("leaf", "mode"), None), P("sep", None, None))
    return jax.shard_map(
        per_device, mesh=mesh, in_specs=in_specs, out_specs=out_specs, check_vma=False
    )
```

```python
import functools

import jax
import jax.numpy as jnp
from jax import lax
from jax.experimental import pallas as pl
from jax.experimental.pallas import tpu as pltpu
from jax.sharding import PartitionSpec as P

SEP_ROWS = 512
IFACE = 256
MODES = 256
COLS = 256
NSEP = 8
LEAF_DEV = 8
PLANE = 16
SIDE = 4
GROUPS = 8
TILES = 18
STRIP = 16
ITERS = 2
epsilon = 1e-06


def project_kernel(coupling_ref, modes_ref, out_ref):
    out_ref[0] = lax.dot_general(
        coupling_ref[0], modes_ref[0], (((0,), (0,)), ((), ())), preferred_element_type=jnp.float32
    ).astype(jnp.bfloat16)


def project(coupling, modes):
    count, rows, columns = coupling.shape
    block = pl.BlockSpec((1, rows, columns), lambda l: (l, 0, 0))
    return pl.pallas_call(
        project_kernel,
        grid=(count,),
        in_specs=[block, block],
        out_specs=pl.BlockSpec((1, columns, columns), lambda l: (l, 0, 0)),
        out_shape=jax.ShapeDtypeStruct((count, columns, columns), jnp.bfloat16),
        compiler_params=pltpu.CompilerParams(vmem_limit_bytes=16 << 20),
        name="project",
    )(*[pltpu.with_memory_space_constraint(x, pltpu.HBM) for x in (coupling, modes)])


def place_of(d, e, place_ref):
    one = (place_ref[1] + d) & (SIDE - 1)
    two = (place_ref[2] + e) & (SIDE - 1)
    return jnp.where(place_ref[0] == 0, two * SIDE + one, one * SIDE + two)


def gram_kernel(
    target_ref, offset_ref, place_ref, own_ref, other_ref, eigen_ref, other_eigen_ref, *refs
):
    out_refs, window_ref, pad_refs = refs[:SIDE], refs[SIDE], refs[SIDE + 1 :]
    core = place_ref[0]
    reach = IFACE + STRIP
    row = lax.broadcasted_iota(jnp.int32, (reach, IFACE), 0)
    column = lax.broadcasted_iota(jnp.int32, (reach, IFACE), 1)
    distance = row - column
    mine, theirs = eigen_ref[...], other_eigen_ref[...]
    eigen = jnp.concatenate(
        [jnp.where(core == 0, mine, theirs), jnp.where(core == 0, theirs, mine)], axis=1
    )
    inverses = 1.0 / jnp.sqrt(eigen)
    starts = [pl.multiple_of(32 * g + 16 * core, STRIP) for g in range(PLANE)]
    window_ref[LEAF_DEV] = jnp.zeros((PLANE, STRIP, 384), jnp.float32)
    for leaf in range(LEAF_DEV):
        product = own_ref[leaf].astype(jnp.float32) + other_ref[leaf].astype(jnp.float32)
        scaled = (product * inverses[leaf : leaf + 1, :]).astype(jnp.bfloat16)
        offset = offset_ref[leaf]
        aligned = pl.multiple_of((offset >> 4) << 4, STRIP)
        placing = (distance == (offset & 15)).astype(jnp.bfloat16)
        pad_ref = pad_refs[leaf]
        pad_ref[...] = jnp.zeros_like(pad_ref)
        pad_ref[pl.ds(aligned, reach), :] = jnp.dot(
            placing, scaled, preferred_element_type=jnp.float32
        ).astype(jnp.bfloat16)
    for leaf in range(LEAF_DEV):
        pad_ref = pad_refs[leaf]
        rows = jnp.concatenate([pad_ref[pl.ds(x, STRIP), :] for x in starts], axis=0)
        total = lax.dot_general(
            rows,
            pad_ref[:SEP_ROWS, :],
            (((1,), (1,)), ((), ())),
            preferred_element_type=jnp.float32,
        )
        for g in range(PLANE):
            strip = total[g * STRIP : (g + 1) * STRIP, :]
            window_ref[leaf, g] = (pltpu.roll(strip, SEP_ROWS - 32 * g, axis=1) if g else strip)[:, :384]
    places = [place_of(k // SIDE, k % SIDE, place_ref) for k in range(PLANE)]
    for s in range(NSEP):
        slots = [jnp.int32(LEAF_DEV), jnp.int32(LEAF_DEV)]
        for leaf in range(LEAF_DEV):
            hit = target_ref[leaf] == s
            later = hit & (slots[0] < LEAF_DEV)
            slots[1] = jnp.where(later, leaf, slots[1])
            slots[0] = jnp.where(hit & jnp.logical_not(later), leaf, slots[0])
        lane = 32 * (s % 4)
        for k in range(PLANE):
            g = places[k]
            out_ref, e = out_refs[k // SIDE], k % SIDE
            window = window_ref[slots[0], g] + window_ref[slots[1], g]
            out_ref[e, 2 * s] = window[:, :128].astype(jnp.bfloat16)
            out_ref[e, 2 * s + 1] = window[:, 128:256].astype(jnp.bfloat16)
            rest = window[:, 256:384]
            rest = pltpu.roll(rest, lane, axis=1) if lane else rest
            out_ref[e, 16 + s // 4, :, lane : lane + 32] = rest[:, lane : lane + 32].astype(
                jnp.bfloat16
            )


def in_vmem(x):
    return pltpu.with_memory_space_constraint(x, pltpu.VMEM)


VMEM = pl.BlockSpec(memory_space=pltpu.VMEM)
SMEM = pl.BlockSpec(memory_space=pltpu.SMEM)


def gram(target, offset, place, *arrays):
    return pl.pallas_call(
        gram_kernel,
        in_specs=[SMEM, SMEM, SMEM, VMEM, VMEM, VMEM, VMEM],
        out_specs=[VMEM] * SIDE,
        out_shape=[jax.ShapeDtypeStruct((SIDE, TILES, STRIP, 128), jnp.bfloat16)] * SIDE,
        scratch_shapes=[
            pltpu.VMEM((LEAF_DEV + 1, PLANE, STRIP, 384), jnp.float32),
            *[pltpu.VMEM((SEP_ROWS + STRIP, MODES), jnp.bfloat16)] * LEAF_DEV,
        ],
        compiler_params=pltpu.CompilerParams(vmem_limit_bytes=24 << 20),
        name="gram",
    )(target, offset, place, *[in_vmem(x) for x in arrays])


def total(refs, *where):
    return sum(ref[where].astype(jnp.float32) for ref in refs).astype(jnp.bfloat16)


def split_kernel(*refs):
    sources, outs = refs[:SIDE], refs[SIDE:]
    for e in range(SIDE):
        for tile in range(TILES):
            outs[e][tile] = total(sources, e, tile)


def route_kernel(*refs):
    sources, out_ref = refs[:SIDE], refs[SIDE]
    for s in range(NSEP):
        out_ref[s, 0] = total(sources, 2 * s)
        out_ref[s, 1] = total(sources, 2 * s + 1)
    for k in range(2):
        rest = total(sources, 16 + k)
        for s in range(4 * k, 4 * k + 4):
            out_ref[s, 2] = rest


def combine(kernel, pieces, shapes):
    return pl.pallas_call(
        kernel,
        in_specs=[VMEM] * SIDE,
        out_specs=[VMEM] * len(shapes),
        out_shape=[jax.ShapeDtypeStruct(shape, jnp.bfloat16) for shape in shapes],
        compiler_params=pltpu.CompilerParams(vmem_limit_bytes=8 << 20),
        name=kernel.__name__,
    )(*[in_vmem(piece) for piece in pieces])


def iterate_kernel(
    place_ref, window_ref, known_ref, known_other_ref, turns_ref, out_ref, norms_ref, kt_ref, m_ref, high_ref, x_ref
):
    core, device, sep = place_ref[0], place_ref[1], place_ref[2]
    leaf = device >> 1
    y, x = leaf >> 2, leaf & 3
    lane = lax.broadcasted_iota(jnp.int32, (STRIP, 128), 1)
    halved = jnp.where(lane < 32, 0.5, 1.0)
    rest_weight = jnp.where(lane < 32, 0.5, 0.0)
    back = (128 - 32 * (sep & 3)) & 127
    for known, which in ((known_ref, core), (known_other_ref, 1 - core)):
        for e in range(SIDE):
            for d in range(SIDE):
                up = (y - jnp.where(which == 0, e, d)) & (SIDE - 1)
                over = (x - jnp.where(which == 0, d, e)) & (SIDE - 1)
                start = 32 * (up * SIDE + over) + 16 * which
                rows = pl.ds(pl.multiple_of(start, STRIP), STRIP)
                kt_ref[rows, :] = known[e, d, :, :SEP_ROWS]
                x_ref[rows, :] = known[e, d, :, SEP_ROWS:]
    for k in range(2 * PLANE):
        rest = pltpu.roll(window_ref[k, :, 256:384].astype(jnp.float32), back, axis=1)
        low = jnp.where(lane < 32, pltpu.roll(rest, 96, axis=1), 0.0)
        first = window_ref[k, :, :128].astype(jnp.float32) + low
        second = window_ref[k, :, 128:256].astype(jnp.float32)
        window = jnp.concatenate(
            [first * halved, second, rest * rest_weight, jnp.zeros_like(second)], axis=1
        )
        shift = 32 * (k // 2)
        m_ref[STRIP * k : STRIP * (k + 1), :] = pltpu.roll(window, shift, axis=1) if shift else window
    half = m_ref[...]
    operator = jnp.transpose(kt_ref[...].astype(jnp.float32) - half) - half
    high = operator.astype(jnp.bfloat16)
    high_ref[...] = high
    error = operator - high.astype(jnp.float32)
    across = lax.broadcasted_iota(jnp.int32, (128, 128), 0)
    along = lax.broadcasted_iota(jnp.int32, (128, 128), 1)
    low = jnp.concatenate(
        [
            jnp.sum(jnp.where(across == along, error[k : k + 128, k : k + 128], 0.0), 1, keepdims=True)
            for k in range(0, SEP_ROWS, 128)
        ],
        axis=0,
    )
    for step in range(ITERS):
        block = x_ref[...]
        summed = jnp.dot(high_ref[...], block, preferred_element_type=jnp.float32)
        summed = summed + low * block.astype(jnp.float32)
        scale = jnp.sqrt(jnp.sum(summed * summed, 0, keepdims=True) / SEP_ROWS + epsilon)
        norms_ref[0, pl.ds(step, 1), :] = scale
        normed = (summed / scale).astype(jnp.bfloat16)
        if step < ITERS - 1:
            x_ref[...] = jnp.dot(
                normed, turns_ref[step], preferred_element_type=jnp.float32
            ).astype(jnp.bfloat16)
        else:
            x_ref[...] = normed
            rows = x_ref[pl.ds(pl.multiple_of(16 * device, STRIP), STRIP), :]
            out_ref[0] = jnp.dot(
                rows, turns_ref[step], preferred_element_type=jnp.float32
            ).astype(jnp.bfloat16)


def iterate(place, *arrays):
    return pl.pallas_call(
        iterate_kernel,
        in_specs=[SMEM] + [VMEM] * len(arrays),
        out_specs=[VMEM, VMEM],
        out_shape=[
            jax.ShapeDtypeStruct((1, STRIP, COLS), jnp.bfloat16),
            jax.ShapeDtypeStruct((1, ITERS, COLS), jnp.float32),
        ],
        scratch_shapes=[
            pltpu.VMEM((SEP_ROWS, SEP_ROWS), jnp.bfloat16),
            pltpu.VMEM((SEP_ROWS, SEP_ROWS), jnp.float32),
            pltpu.VMEM((SEP_ROWS, SEP_ROWS), jnp.bfloat16),
            pltpu.VMEM((SEP_ROWS, COLS), jnp.bfloat16),
        ],
        compiler_params=pltpu.CompilerParams(vmem_limit_bytes=16 << 20),
        name="iterate",
    )(place, *[in_vmem(array) for array in arrays])


SWAP = [(0, 1), (1, 0)]
AXES = ("leaf", "sep", "mode")


def index_of(y, x, z, core):
    return ((y * SIDE + x) * GROUPS + z) * 2 + core


def plane_steps(step, stage):
    pairs = []
    for y in range(SIDE):
        for x in range(SIDE):
            for z in range(GROUPS):
                for core in range(2):
                    along_x = (core + stage) % 2 == 0
                    to = (y, (x + step) % SIDE) if along_x else ((y + step) % SIDE, x)
                    pairs.append((index_of(y, x, z, core), index_of(*to, z, core)))
    return pairs


def after(value, earlier):
    return lax.optimization_barrier((value, earlier))[0]


def gather_stage(value, stage):
    got = [lax.ppermute(value, AXES, plane_steps(d, stage)) for d in ORDER]
    return jnp.stack([value, got[0], got[2], got[1]])


def scatter_stage(pieces, stage):
    got = [lax.ppermute(pieces[d], AXES, plane_steps(d, stage)) for d in ORDER]
    return [pieces[0], *got]


ORDER = (1, 3, 2)

def per_device(
    modes, coupling, eigenvalues, separator_of, row_offset, stiffness, start_block, rotations
):
    core = lax.axis_index("mode").astype(jnp.int32)
    device = lax.axis_index(("leaf", "mode")).astype(jnp.int32)
    other_eigen = lax.ppermute(eigenvalues, "mode", SWAP)
    own = project(coupling, modes)
    other = lax.ppermute(own, "mode", SWAP)
    sep = lax.axis_index("sep").astype(jnp.int32)
    leaf = lax.axis_index("leaf").astype(jnp.int32)
    y, x = leaf >> 2, leaf & 3
    place = jnp.stack([core, jnp.where(core == 0, x, y), jnp.where(core == 0, y, x)])
    pieces = gram(separator_of[:, 0], row_offset, place, own, other, eigenvalues, other_eigen)
    piece = (TILES, STRIP, 128)
    known = jnp.concatenate([stiffness[0].T, start_block[0]], 1)
    near = gather_stage(after(known, pieces[0]), 0)
    pieces = combine(split_kernel, scatter_stage(pieces, 0), [piece] * SIDE)
    known = gather_stage(after(near, pieces[0]), 1)
    (routed,) = combine(route_kernel, scatter_stage(pieces, 1), [(NSEP, 3, STRIP, 128)])
    known_other = lax.ppermute(after(known, routed), "mode", SWAP)
    got = lax.all_to_all(routed, "sep", split_axis=0, concat_axis=0, tiled=True)
    window = jnp.sum(got.astype(jnp.float32), 0)
    high = window.astype(jnp.bfloat16)
    low = (window[0] - high[0].astype(jnp.float32)).astype(jnp.bfloat16)
    group = lax.broadcasted_iota(jnp.int32, (STRIP, 128), 1) >> 5
    rest = jnp.where(group == (sep & 3), high[2], jnp.concatenate([low[:, :32]] * 4, 1))
    packed = jnp.concatenate([high[0], high[1], rest], 1)
    windows = lax.all_to_all(
        jnp.broadcast_to(packed[None], (2 * PLANE, *packed.shape)),
        ("leaf", "mode"),
        split_axis=0,
        concat_axis=0,
        tiled=True,
    )
    place = jnp.stack([core, device, sep])
    return tuple(iterate(place, windows, known, known_other, rotations[0]))


def solution(mesh):
    in_specs = (
        P(("leaf", "sep"), "mode", None),
        P(("leaf", "sep"), "mode", None),
        P(("leaf", "sep"), "mode"),
        P(("leaf", "sep"), None),
        P(("leaf", "sep")),
        P("sep", None, ("leaf", "mode")),
        P("sep", ("leaf", "mode"), None),
        P("sep", None, None, None),
    )
    out_specs = (P("sep", ("leaf", "mode"), None), P("sep", None, None))
    return jax.shard_map(
        per_device, mesh=mesh, in_specs=in_specs, out_specs=out_specs, check_vma=False
    )
```

```python
import functools

import jax
import jax.numpy as jnp
from jax import lax
from jax.experimental import pallas as pl
from jax.experimental.pallas import tpu as pltpu
from jax.sharding import PartitionSpec as P

SEP_ROWS = 512
IFACE = 256
MODES = 256
COLS = 256
NSEP = 8
LEAF_DEV = 8
PLANE = 16
SIDE = 4
GROUPS = 8
TILES = 18
STRIP = 16
ITERS = 2
epsilon = 1e-06


def position():
    leaf = lax.axis_index("leaf").astype(jnp.int32)
    return leaf >> 2, leaf & (SIDE - 1), lax.axis_index("mode").astype(jnp.int32)


def place_of(d, e, place_ref):
    one = (place_ref[1] + d) & (SIDE - 1)
    two = (place_ref[2] + e) & (SIDE - 1)
    return jnp.where(place_ref[0] == 0, two * SIDE + one, one * SIDE + two)


def gram_kernel(
    target_ref, offset_ref, place_ref, own_ref, other_ref, eigen_ref, other_eigen_ref, *refs
):
    out_refs, window_ref, pad_refs = refs[:SIDE], refs[SIDE], refs[SIDE + 1 :]
    core = place_ref[0]
    reach = IFACE + STRIP
    row = lax.broadcasted_iota(jnp.int32, (reach, IFACE), 0)
    column = lax.broadcasted_iota(jnp.int32, (reach, IFACE), 1)
    distance = row - column
    mine, theirs = eigen_ref[...], other_eigen_ref[...]
    eigen = jnp.concatenate(
        [jnp.where(core == 0, mine, theirs), jnp.where(core == 0, theirs, mine)], axis=1
    )
    inverses = 1.0 / jnp.sqrt(eigen)
    starts = [pl.multiple_of(32 * g + 16 * core, STRIP) for g in range(PLANE)]
    window_ref[LEAF_DEV] = jnp.zeros((PLANE, STRIP, 384), jnp.float32)
    for leaf in range(LEAF_DEV):
        product = own_ref[leaf].astype(jnp.float32) + other_ref[leaf].astype(jnp.float32)
        scaled = (product * inverses[leaf : leaf + 1, :]).astype(jnp.bfloat16)
        offset = offset_ref[leaf]
        aligned = pl.multiple_of((offset >> 4) << 4, STRIP)
        placing = (distance == (offset & 15)).astype(jnp.bfloat16)
        pad_ref = pad_refs[leaf]
        pad_ref[...] = jnp.zeros_like(pad_ref)
        pad_ref[pl.ds(aligned, reach), :] = jnp.dot(
            placing, scaled, preferred_element_type=jnp.float32
        ).astype(jnp.bfloat16)
    for leaf in range(LEAF_DEV):
        pad_ref = pad_refs[leaf]
        rows = jnp.concatenate([pad_ref[pl.ds(x, STRIP), :] for x in starts], axis=0)
        total = lax.dot_general(
            rows,
            pad_ref[:SEP_ROWS, :],
            (((1,), (1,)), ((), ())),
            preferred_element_type=jnp.float32,
        )
        for g in range(PLANE):
            strip = total[g * STRIP : (g + 1) * STRIP, :]
            window_ref[leaf, g] = (pltpu.roll(strip, SEP_ROWS - 32 * g, axis=1) if g else strip)[:, :384]
    places = [place_of(k // SIDE, k % SIDE, place_ref) for k in range(PLANE)]
    for s in range(NSEP):
        slots = [jnp.int32(LEAF_DEV), jnp.int32(LEAF_DEV)]
        for leaf in range(LEAF_DEV):
            hit = target_ref[leaf] == s
            later = hit & (slots[0] < LEAF_DEV)
            slots[1] = jnp.where(later, leaf, slots[1])
            slots[0] = jnp.where(hit & jnp.logical_not(later), leaf, slots[0])
        lane = 32 * (s % 4)
        for k in range(PLANE):
            g = places[k]
            out_ref, e = out_refs[k // SIDE], k % SIDE
            window = window_ref[slots[0], g] + window_ref[slots[1], g]
            out_ref[e, 2 * s] = window[:, :128].astype(jnp.bfloat16)
            out_ref[e, 2 * s + 1] = window[:, 128:256].astype(jnp.bfloat16)
            rest = window[:, 256:384]
            rest = pltpu.roll(rest, lane, axis=1) if lane else rest
            out_ref[e, 16 + s // 4, :, lane : lane + 32] = rest[:, lane : lane + 32].astype(
                jnp.bfloat16
            )


def in_vmem(x):
    return pltpu.with_memory_space_constraint(x, pltpu.VMEM)


VMEM = pl.BlockSpec(memory_space=pltpu.VMEM)
SMEM = pl.BlockSpec(memory_space=pltpu.SMEM)


def gram(target, offset, place, *arrays):
    return pl.pallas_call(
        gram_kernel,
        in_specs=[SMEM, SMEM, SMEM, VMEM, VMEM, VMEM, VMEM],
        out_specs=[VMEM] * SIDE,
        out_shape=[jax.ShapeDtypeStruct((SIDE, TILES, STRIP, 128), jnp.bfloat16)] * SIDE,
        scratch_shapes=[
            pltpu.VMEM((LEAF_DEV + 1, PLANE, STRIP, 384), jnp.float32),
            *[pltpu.VMEM((SEP_ROWS + STRIP, MODES), jnp.bfloat16)] * LEAF_DEV,
        ],
        compiler_params=pltpu.CompilerParams(vmem_limit_bytes=24 << 20),
        name="gram",
    )(target, offset, place, *[in_vmem(x) for x in arrays])


def total(refs, *where):
    return sum(ref[where].astype(jnp.float32) for ref in refs).astype(jnp.bfloat16)


def split_kernel(*refs):
    sources, outs = refs[:SIDE], refs[SIDE:]
    for e in range(SIDE):
        for tile in range(TILES):
            outs[e][tile] = total(sources, e, tile)


def route_kernel(*refs):
    sources, out_ref = refs[:SIDE], refs[SIDE]
    for s in range(NSEP):
        out_ref[s, 0] = total(sources, 2 * s)
        out_ref[s, 1] = total(sources, 2 * s + 1)
    for k in range(2):
        rest = total(sources, 16 + k)
        for s in range(4 * k, 4 * k + 4):
            out_ref[s, 2] = rest


def combine(kernel, pieces, shapes):
    return pl.pallas_call(
        kernel,
        in_specs=[VMEM] * SIDE,
        out_specs=[VMEM] * len(shapes),
        out_shape=[jax.ShapeDtypeStruct(shape, jnp.bfloat16) for shape in shapes],
        compiler_params=pltpu.CompilerParams(vmem_limit_bytes=8 << 20),
        name=kernel.__name__,
    )(*[in_vmem(piece) for piece in pieces])


def iterate_kernel(
    own_ref, other_ref, known_ref, known_other_ref, turns_ref, out_hbm, norms_hbm, kt_ref, m_ref, high_ref, x_ref, out_ref, norms_ref, sems
):
    y, x, core = position()
    device = 2 * (y * SIDE + x) + core
    sep = lax.axis_index("sep").astype(jnp.int32)
    lane = lax.broadcasted_iota(jnp.int32, (STRIP, 128), 1)
    halved = jnp.where(lane < 32, 0.5, 1.0)
    rest_weight = jnp.where(lane < 32, 0.5, 0.0)
    back = (128 - 32 * (sep & 3)) & 127
    for ref, known, which in ((own_ref, known_ref, core), (other_ref, known_other_ref, 1 - core)):
        for e in range(SIDE):
            for d in range(SIDE):
                up = (y - jnp.where(which == 0, e, d)) & (SIDE - 1)
                over = (x - jnp.where(which == 0, d, e)) & (SIDE - 1)
                start = 32 * (up * SIDE + over) + 16 * which
                rows = pl.ds(pl.multiple_of(start, STRIP), STRIP)
                kt_ref[rows, :] = known[e, d, :, :SEP_ROWS]
                x_ref[rows, :] = known[e, d, :, SEP_ROWS:]
        for g in range(PLANE):
            rows = pl.ds(pl.multiple_of(32 * g + 16 * which, STRIP), STRIP)
            rest = pltpu.roll(ref[g, :, 256:384].astype(jnp.float32), back, axis=1)
            low = jnp.where(lane < 32, pltpu.roll(rest, 96, axis=1), 0.0)
            first = ref[g, :, :128].astype(jnp.float32) + low
            second = ref[g, :, 128:256].astype(jnp.float32)
            window = jnp.concatenate(
                [first * halved, second, rest * rest_weight, jnp.zeros_like(second)], axis=1
            )
            m_ref[rows, :] = pltpu.roll(window, 32 * g, axis=1) if g else window
    half = m_ref[...]
    operator = jnp.transpose(kt_ref[...].astype(jnp.float32) - half) - half
    high = operator.astype(jnp.bfloat16)
    high_ref[...] = high
    error = operator - high.astype(jnp.float32)
    across = lax.broadcasted_iota(jnp.int32, (128, 128), 0)
    along = lax.broadcasted_iota(jnp.int32, (128, 128), 1)
    low = jnp.concatenate(
        [
            jnp.sum(jnp.where(across == along, error[k : k + 128, k : k + 128], 0.0), 1, keepdims=True)
            for k in range(0, SEP_ROWS, 128)
        ],
        axis=0,
    )
    for step in range(ITERS):
        block = x_ref[...]
        summed = jnp.dot(high_ref[...], block, preferred_element_type=jnp.float32)
        summed = summed + low * block.astype(jnp.float32)
        scale = jnp.sqrt(jnp.sum(summed * summed, 0, keepdims=True) / SEP_ROWS + epsilon)
        norms_ref[0, pl.ds(step, 1), :] = scale
        normed = (summed * (1.0 / scale)).astype(jnp.bfloat16)
        if step < ITERS - 1:
            x_ref[...] = jnp.dot(
                normed, turns_ref[step], preferred_element_type=jnp.float32
            ).astype(jnp.bfloat16)
        else:
            norms_copy = pltpu.make_async_copy(norms_ref, norms_hbm, sems.at[0])
            norms_copy.start()
            x_ref[...] = normed
            rows = x_ref[pl.ds(pl.multiple_of(16 * device, STRIP), STRIP), :]
            out_ref[0] = jnp.dot(
                rows, turns_ref[step], preferred_element_type=jnp.float32
            ).astype(jnp.bfloat16)
            out_copy = pltpu.make_async_copy(out_ref, out_hbm, sems.at[1])
            out_copy.start()
            norms_copy.wait()
            out_copy.wait()


def iterate(*arrays):
    return pl.pallas_call(
        iterate_kernel,
        in_specs=[VMEM] * len(arrays),
        out_specs=[pl.BlockSpec(memory_space=pltpu.HBM)] * 2,
        out_shape=[
            jax.ShapeDtypeStruct((1, STRIP, COLS), jnp.bfloat16),
            jax.ShapeDtypeStruct((1, ITERS, COLS), jnp.float32),
        ],
        scratch_shapes=[
            pltpu.VMEM((SEP_ROWS, SEP_ROWS), jnp.bfloat16),
            pltpu.VMEM((SEP_ROWS, SEP_ROWS), jnp.float32),
            pltpu.VMEM((SEP_ROWS, SEP_ROWS), jnp.bfloat16),
            pltpu.VMEM((SEP_ROWS, COLS), jnp.bfloat16),
            pltpu.VMEM((1, STRIP, COLS), jnp.bfloat16),
            pltpu.VMEM((1, ITERS, COLS), jnp.float32),
            pltpu.SemaphoreType.DMA((2,)),
        ],
        compiler_params=pltpu.CompilerParams(vmem_limit_bytes=16 << 20),
        name="iterate",
    )(*[in_vmem(array) for array in arrays])


SWAP = [(0, 1), (1, 0)]
AXES = ("leaf", "sep", "mode")


def index_of(y, x, z, core):
    return ((y * SIDE + x) * GROUPS + z) * 2 + core


def plane_steps(step, stage):
    pairs = []
    for y in range(SIDE):
        for x in range(SIDE):
            for z in range(GROUPS):
                for core in range(2):
                    along_x = (core + stage) % 2 == 0
                    to = (y, (x + step) % SIDE) if along_x else ((y + step) % SIDE, x)
                    pairs.append((index_of(y, x, z, core), index_of(*to, z, core)))
    return pairs


def after(value, earlier):
    return lax.optimization_barrier((value, earlier))[0]


def gather_stage(value, stage):
    got = [lax.ppermute(value, AXES, plane_steps(d, stage)) for d in ORDER]
    return jnp.stack([value, got[0], got[2], got[1]])


def scatter_stage(pieces, stage):
    got = [lax.ppermute(pieces[d], AXES, plane_steps(d, stage)) for d in ORDER]
    return [pieces[0], *got]


ORDER = (1, 3, 2)

def per_device(
    modes, coupling, eigenvalues, separator_of, row_offset, stiffness, start_block, rotations
):
    other_eigen = lax.ppermute(eigenvalues, "mode", SWAP)
    own = jnp.einsum("ldw,ldm->lwm", coupling, modes, preferred_element_type=jnp.float32).astype(
        jnp.bfloat16
    )
    other = lax.ppermute(own, "mode", SWAP)
    sep = lax.axis_index("sep").astype(jnp.int32)
    y, x, core = position()
    place = jnp.stack([core, jnp.where(core == 0, x, y), jnp.where(core == 0, y, x)])
    pieces = gram(separator_of[:, 0], row_offset, place, own, other, eigenvalues, other_eigen)
    piece = (TILES, STRIP, 128)
    known = jnp.concatenate([stiffness[0].T, start_block[0]], 1)
    near = gather_stage(after(known, pieces[0]), 0)
    pieces = combine(split_kernel, scatter_stage(pieces, 0), [piece] * SIDE)
    known = gather_stage(after(near, pieces[0]), 1)
    (routed,) = combine(route_kernel, scatter_stage(pieces, 1), [(NSEP, 3, STRIP, 128)])
    known_other = lax.ppermute(after(known, routed), "mode", SWAP)
    got = lax.all_to_all(routed, "sep", split_axis=0, concat_axis=0, tiled=True)
    window = jnp.sum(got.astype(jnp.float32), 0)
    high = window.astype(jnp.bfloat16)
    low = (window[0] - high[0].astype(jnp.float32)).astype(jnp.bfloat16)
    group = lax.broadcasted_iota(jnp.int32, (STRIP, 128), 1) >> 5
    rest = jnp.where(group == (sep & 3), high[2], jnp.concatenate([low[:, :32]] * 4, 1))
    packed = jnp.concatenate([high[0], high[1], rest], 1)
    mine = lax.all_to_all(
        jnp.broadcast_to(packed[None], (PLANE, *packed.shape)),
        "leaf",
        split_axis=0,
        concat_axis=0,
        tiled=True,
    )
    theirs = lax.ppermute(mine, "mode", SWAP)
    return tuple(iterate(mine, theirs, known, known_other, rotations[0]))


def solution(mesh):
    in_specs = (
        P(("leaf", "sep"), "mode", None),
        P(("leaf", "sep"), "mode", None),
        P(("leaf", "sep"), "mode"),
        P(("leaf", "sep"), None),
        P(("leaf", "sep")),
        P("sep", None, ("leaf", "mode")),
        P("sep", ("leaf", "mode"), None),
        P("sep", None, None, None),
    )
    out_specs = (P("sep", ("leaf", "mode"), None), P("sep", None, None))
    return jax.shard_map(
        per_device, mesh=mesh, in_specs=in_specs, out_specs=out_specs, check_vma=False
    )
```

```python
import functools

import jax
import jax.numpy as jnp
from jax import lax
from jax.experimental import pallas as pl
from jax.experimental.pallas import tpu as pltpu
from jax.sharding import PartitionSpec as P

SEP_ROWS = 512
IFACE = 256
MODES = 256
COLS = 256
NSEP = 8
LEAF_DEV = 8
PLANE = 16
SIDE = 4
GROUPS = 8
TILES = 18
STRIP = 16
ITERS = 2
epsilon = 1e-06


def position():
    leaf = lax.axis_index("leaf").astype(jnp.int32)
    return leaf >> 2, leaf & (SIDE - 1), lax.axis_index("mode").astype(jnp.int32)


def place_of(d, e, place_ref):
    one = (place_ref[1] + d) & (SIDE - 1)
    two = (place_ref[2] + e) & (SIDE - 1)
    return jnp.where(place_ref[0] == 0, two * SIDE + one, one * SIDE + two)


def gram_kernel(
    target_ref, offset_ref, place_ref, own_ref, other_ref, eigen_ref, other_eigen_ref, *refs
):
    out_refs, window_ref, pad_refs = refs[:SIDE], refs[SIDE], refs[SIDE + 1 :]
    core = place_ref[0]
    reach = IFACE + STRIP
    row = lax.broadcasted_iota(jnp.int32, (reach, IFACE), 0)
    column = lax.broadcasted_iota(jnp.int32, (reach, IFACE), 1)
    distance = row - column
    mine, theirs = eigen_ref[...], other_eigen_ref[...]
    eigen = jnp.concatenate(
        [jnp.where(core == 0, mine, theirs), jnp.where(core == 0, theirs, mine)], axis=1
    )
    inverses = 1.0 / jnp.sqrt(eigen)
    starts = [pl.multiple_of(32 * g + 16 * core, STRIP) for g in range(PLANE)]
    window_ref[LEAF_DEV] = jnp.zeros((PLANE, STRIP, 384), jnp.float32)
    for leaf in range(LEAF_DEV):
        product = own_ref[leaf].astype(jnp.float32) + other_ref[leaf].astype(jnp.float32)
        scaled = (product * inverses[leaf : leaf + 1, :]).astype(jnp.bfloat16)
        offset = offset_ref[leaf]
        aligned = pl.multiple_of((offset >> 4) << 4, STRIP)
        placing = (distance == (offset & 15)).astype(jnp.bfloat16)
        pad_ref = pad_refs[leaf]
        pad_ref[...] = jnp.zeros_like(pad_ref)
        pad_ref[pl.ds(aligned, reach), :] = jnp.dot(
            placing, scaled, preferred_element_type=jnp.float32
        ).astype(jnp.bfloat16)
    for leaf in range(LEAF_DEV):
        pad_ref = pad_refs[leaf]
        rows = jnp.concatenate([pad_ref[pl.ds(x, STRIP), :] for x in starts], axis=0)
        total = lax.dot_general(
            rows,
            pad_ref[:SEP_ROWS, :],
            (((1,), (1,)), ((), ())),
            preferred_element_type=jnp.float32,
        )
        for g in range(PLANE):
            strip = total[g * STRIP : (g + 1) * STRIP, :]
            window_ref[leaf, g] = (pltpu.roll(strip, SEP_ROWS - 32 * g, axis=1) if g else strip)[:, :384]
    places = [place_of(k // SIDE, k % SIDE, place_ref) for k in range(PLANE)]
    for s in range(NSEP):
        slots = [jnp.int32(LEAF_DEV), jnp.int32(LEAF_DEV)]
        for leaf in range(LEAF_DEV):
            hit = target_ref[leaf] == s
            later = hit & (slots[0] < LEAF_DEV)
            slots[1] = jnp.where(later, leaf, slots[1])
            slots[0] = jnp.where(hit & jnp.logical_not(later), leaf, slots[0])
        lane = 32 * (s % 4)
        for k in range(PLANE):
            g = places[k]
            out_ref, e = out_refs[k // SIDE], k % SIDE
            window = window_ref[slots[0], g] + window_ref[slots[1], g]
            out_ref[e, 2 * s] = window[:, :128].astype(jnp.bfloat16)
            out_ref[e, 2 * s + 1] = window[:, 128:256].astype(jnp.bfloat16)
            rest = window[:, 256:384]
            rest = pltpu.roll(rest, lane, axis=1) if lane else rest
            out_ref[e, 16 + s // 4, :, lane : lane + 32] = rest[:, lane : lane + 32].astype(
                jnp.bfloat16
            )


def in_vmem(x):
    return pltpu.with_memory_space_constraint(x, pltpu.VMEM)


VMEM = pl.BlockSpec(memory_space=pltpu.VMEM)
SMEM = pl.BlockSpec(memory_space=pltpu.SMEM)


def gram(target, offset, place, *arrays):
    return pl.pallas_call(
        gram_kernel,
        in_specs=[SMEM, SMEM, SMEM, VMEM, VMEM, VMEM, VMEM],
        out_specs=[VMEM] * SIDE,
        out_shape=[jax.ShapeDtypeStruct((SIDE, TILES, STRIP, 128), jnp.bfloat16)] * SIDE,
        scratch_shapes=[
            pltpu.VMEM((LEAF_DEV + 1, PLANE, STRIP, 384), jnp.float32),
            *[pltpu.VMEM((SEP_ROWS + STRIP, MODES), jnp.bfloat16)] * LEAF_DEV,
        ],
        compiler_params=pltpu.CompilerParams(vmem_limit_bytes=24 << 20),
        name="gram",
    )(target, offset, place, *[in_vmem(x) for x in arrays])


def total(refs, *where):
    return sum(ref[where].astype(jnp.float32) for ref in refs).astype(jnp.bfloat16)


def split_kernel(*refs):
    sources, outs = refs[:SIDE], refs[SIDE:]
    for e in range(SIDE):
        for tile in range(TILES):
            outs[e][tile] = total(sources, e, tile)


def route_kernel(*refs):
    sources, out_ref = refs[:SIDE], refs[SIDE]
    for s in range(NSEP):
        out_ref[s, 0] = total(sources, 2 * s)
        out_ref[s, 1] = total(sources, 2 * s + 1)
    for k in range(2):
        rest = total(sources, 16 + k)
        for s in range(4 * k, 4 * k + 4):
            out_ref[s, 2] = rest


def combine(kernel, pieces, shapes):
    return pl.pallas_call(
        kernel,
        in_specs=[VMEM] * SIDE,
        out_specs=[VMEM] * len(shapes),
        out_shape=[jax.ShapeDtypeStruct(shape, jnp.bfloat16) for shape in shapes],
        compiler_params=pltpu.CompilerParams(vmem_limit_bytes=8 << 20),
        name=kernel.__name__,
    )(*[in_vmem(piece) for piece in pieces])


def iterate_kernel(
    own_ref, other_ref, known_ref, known_other_ref, turns_ref, out_hbm, norms_hbm, kt_ref, m_ref, high_ref, x_ref, out_ref, norms_ref, sems
):
    y, x, core = position()
    device = 2 * (y * SIDE + x) + core
    sep = lax.axis_index("sep").astype(jnp.int32)
    lane = lax.broadcasted_iota(jnp.int32, (STRIP, 128), 1)
    halved = jnp.where(lane < 32, 0.5, 1.0)
    rest_weight = jnp.where(lane < 32, 0.5, 0.0)
    back = (128 - 32 * (sep & 3)) & 127
    for ref, known, which in ((own_ref, known_ref, core), (other_ref, known_other_ref, 1 - core)):
        for e in range(SIDE):
            for d in range(SIDE):
                up = (y - jnp.where(which == 0, e, d)) & (SIDE - 1)
                over = (x - jnp.where(which == 0, d, e)) & (SIDE - 1)
                start = 32 * (up * SIDE + over) + 16 * which
                rows = pl.ds(pl.multiple_of(start, STRIP), STRIP)
                kt_ref[rows, :] = known[e, d, :, :SEP_ROWS]
                x_ref[rows, :] = known[e, d, :, SEP_ROWS:]
        for g in range(PLANE):
            rows = pl.ds(pl.multiple_of(32 * g + 16 * which, STRIP), STRIP)
            rest = pltpu.roll(ref[g, :, 256:384].astype(jnp.float32), back, axis=1)
            low = jnp.where(lane < 32, pltpu.roll(rest, 96, axis=1), 0.0)
            first = ref[g, :, :128].astype(jnp.float32) + low
            second = ref[g, :, 128:256].astype(jnp.float32)
            window = jnp.concatenate(
                [first * halved, second, rest * rest_weight, jnp.zeros_like(second)], axis=1
            )
            m_ref[rows, :] = pltpu.roll(window, 32 * g, axis=1) if g else window
    half = m_ref[...]
    operator = jnp.transpose(kt_ref[...].astype(jnp.float32) - half) - half
    high = operator.astype(jnp.bfloat16)
    high_ref[...] = high
    error = operator - high.astype(jnp.float32)
    across = lax.broadcasted_iota(jnp.int32, (128, 128), 0)
    along = lax.broadcasted_iota(jnp.int32, (128, 128), 1)
    low = jnp.concatenate(
        [
            jnp.sum(jnp.where(across == along, error[k : k + 128, k : k + 128], 0.0), 1, keepdims=True)
            for k in range(0, SEP_ROWS, 128)
        ],
        axis=0,
    )
    for step in range(ITERS):
        block = x_ref[...]
        summed = jnp.dot(high_ref[...], block, preferred_element_type=jnp.float32)
        summed = summed + low * block.astype(jnp.float32)
        scale = jnp.sqrt(jnp.sum(summed * summed, 0, keepdims=True) / SEP_ROWS + epsilon)
        norms_ref[0, pl.ds(step, 1), :] = scale
        normed = (summed * (1.0 / scale)).astype(jnp.bfloat16)
        if step < ITERS - 1:
            x_ref[...] = jnp.dot(
                normed, turns_ref[step], preferred_element_type=jnp.float32
            ).astype(jnp.bfloat16)
        else:
            norms_copy = pltpu.make_async_copy(norms_ref, norms_hbm, sems.at[0])
            norms_copy.start()
            x_ref[...] = normed
            rows = x_ref[pl.ds(pl.multiple_of(16 * device, STRIP), STRIP), :]
            out_ref[0] = jnp.dot(
                rows, turns_ref[step], preferred_element_type=jnp.float32
            ).astype(jnp.bfloat16)
            out_copy = pltpu.make_async_copy(out_ref, out_hbm, sems.at[1])
            out_copy.start()
            norms_copy.wait()
            out_copy.wait()


def iterate(*arrays):
    return pl.pallas_call(
        iterate_kernel,
        in_specs=[VMEM] * len(arrays),
        out_specs=[pl.BlockSpec(memory_space=pltpu.HBM)] * 2,
        out_shape=[
            jax.ShapeDtypeStruct((1, STRIP, COLS), jnp.bfloat16),
            jax.ShapeDtypeStruct((1, ITERS, COLS), jnp.float32),
        ],
        scratch_shapes=[
            pltpu.VMEM((SEP_ROWS, SEP_ROWS), jnp.bfloat16),
            pltpu.VMEM((SEP_ROWS, SEP_ROWS), jnp.float32),
            pltpu.VMEM((SEP_ROWS, SEP_ROWS), jnp.bfloat16),
            pltpu.VMEM((SEP_ROWS, COLS), jnp.bfloat16),
            pltpu.VMEM((1, STRIP, COLS), jnp.bfloat16),
            pltpu.VMEM((1, ITERS, COLS), jnp.float32),
            pltpu.SemaphoreType.DMA((2,)),
        ],
        compiler_params=pltpu.CompilerParams(vmem_limit_bytes=16 << 20),
        name="iterate",
    )(*[in_vmem(array) for array in arrays])


SWAP = [(0, 1), (1, 0)]
AXES = ("leaf", "sep", "mode")


def index_of(y, x, z, core):
    return ((y * SIDE + x) * GROUPS + z) * 2 + core


def plane_steps(step, stage):
    pairs = []
    for y in range(SIDE):
        for x in range(SIDE):
            for z in range(GROUPS):
                for core in range(2):
                    along_x = (core + stage) % 2 == 0
                    to = (y, (x + step) % SIDE) if along_x else ((y + step) % SIDE, x)
                    pairs.append((index_of(y, x, z, core), index_of(*to, z, core)))
    return pairs


def after(value, earlier):
    return lax.optimization_barrier((value, earlier))[0]


def gather_stage(value, stage):
    got = [lax.ppermute(value, AXES, plane_steps(d, stage)) for d in ORDER]
    return jnp.stack([value, got[0], got[2], got[1]])


def scatter_stage(pieces, stage):
    got = [lax.ppermute(pieces[d], AXES, plane_steps(d, stage)) for d in (2, 1, 3)]
    return [pieces[0], *got]


ORDER = (1, 3, 2)

def per_device(
    modes, coupling, eigenvalues, separator_of, row_offset, stiffness, start_block, rotations
):
    other_eigen = lax.ppermute(eigenvalues, "mode", SWAP)
    own = jnp.einsum("ldw,ldm->lwm", coupling, modes, preferred_element_type=jnp.float32).astype(
        jnp.bfloat16
    )
    other = lax.ppermute(own, "mode", SWAP)
    sep = lax.axis_index("sep").astype(jnp.int32)
    y, x, core = position()
    place = jnp.stack([core, jnp.where(core == 0, x, y), jnp.where(core == 0, y, x)])
    pieces = gram(separator_of[:, 0], row_offset, place, own, other, eigenvalues, other_eigen)
    piece = (TILES, STRIP, 128)
    known = jnp.concatenate([stiffness[0].T, start_block[0]], 1)
    near = gather_stage(after(known, pieces[0]), 0)
    pieces = combine(split_kernel, scatter_stage(pieces, 0), [piece] * SIDE)
    known = gather_stage(after(near, pieces[0]), 1)
    (routed,) = combine(route_kernel, scatter_stage(pieces, 1), [(NSEP, 3, STRIP, 128)])
    known_other = lax.ppermute(after(known, routed), "mode", SWAP)
    got = lax.all_to_all(routed, "sep", split_axis=0, concat_axis=0, tiled=True)
    window = jnp.sum(got.astype(jnp.float32), 0)
    high = window.astype(jnp.bfloat16)
    low = (window[0] - high[0].astype(jnp.float32)).astype(jnp.bfloat16)
    group = lax.broadcasted_iota(jnp.int32, (STRIP, 128), 1) >> 5
    rest = jnp.where(group == (sep & 3), high[2], jnp.concatenate([low[:, :32]] * 4, 1))
    packed = jnp.concatenate([high[0], high[1], rest], 1)
    mine = lax.all_to_all(
        jnp.broadcast_to(packed[None], (PLANE, *packed.shape)),
        "leaf",
        split_axis=0,
        concat_axis=0,
        tiled=True,
    )
    theirs = lax.ppermute(mine, "mode", SWAP)
    return tuple(iterate(mine, theirs, known, known_other, rotations[0]))


def solution(mesh):
    in_specs = (
        P(("leaf", "sep"), "mode", None),
        P(("leaf", "sep"), "mode", None),
        P(("leaf", "sep"), "mode"),
        P(("leaf", "sep"), None),
        P(("leaf", "sep")),
        P("sep", None, ("leaf", "mode")),
        P("sep", ("leaf", "mode"), None),
        P("sep", None, None, None),
    )
    out_specs = (P("sep", ("leaf", "mode"), None), P("sep", None, None))
    return jax.shard_map(
        per_device, mesh=mesh, in_specs=in_specs, out_specs=out_specs, check_vma=False
    )
```
